32 devices in a mesh: seq: 32 (over z, y, x, core).
Axes of the slice: x: 2, y: 2, z: 4, core: 2. Of those that a mesh axis runs over, the one named last changes fastest.
Arguments:
- queries: bfloat16 [8192, 2048], P('seq'), may hold values from -30 to 30
- keys: bfloat16 [8192, 2048], P('seq'), may hold values from -9 to 9
- values: bfloat16 [8192, 2048], P('seq'), may hold values from -6 to 6
- grad_out: bfloat16 [8192, 2048], P('seq'), may hold values from -6 to 6
- proj_weight: bfloat16 [16, 128, 256], replicated, may hold values from -2.734375 to 2.734375
Outputs:
- grad_queries: bfloat16 [8192, 2048], P('seq')
- grad_keys: bfloat16 [8192, 2048], P('seq')
- grad_values: bfloat16 [8192, 2048], P('seq')
- grad_proj: float32 [2048, 256], P('seq')
The draws below stay inside these ranges and needn't reach their ends.
All inputs are finite; a program needn't handle non-finite values.
Results may differ from the reference program's by a relative error of at most 0.01.
Values may be sent and summed in bfloat16 or wider, within the bound.
No kernel may reach another device: no remote copies, remote signals or barrier semaphores. Data moves between devices by JAX's collectives and lax.ppermute only.
A program may use at most 128 MiB of HBM per device.

```python
import math
import jax
import jax.numpy as jnp
from jax import lax

HEADS = 16
HEAD_DIM = 128
RANK = 256
SEG = 256
TOKENS = 8192


def drawn_rows():
    return [TOKENS // 2 + 11 + step * (TOKENS // 8) for step in range(3)]


def key_layout(key):
    base = jax.random.fold_in(key, 7)
    width_all = HEADS * HEAD_DIM
    rows = jnp.arange(TOKENS, dtype=jnp.int32)[:, None]
    place = rows.astype(jnp.float32) / TOKENS
    offset = rows - 37
    attend_lead = (offset >= 0) & (offset % 2018 == 0) & (rows + 2 < TOKENS)
    strength = 10.0 + 10.0 * (offset // 2018 % 3).astype(jnp.float32)
    gap_rows = jnp.where(attend_lead, 2.0 / (math.sqrt(HEAD_DIM) * strength), 0.0)
    proj_lead = jnp.zeros((TOKENS, 1), dtype=bool)
    proj_strength = [120.0, 250.0, 350.0]
    for step, row_at in enumerate(drawn_rows()):
        hit = rows == row_at
        proj_lead = proj_lead | hit
        gap_rows = jnp.where(hit, 2.0 / proj_strength[step], gap_rows)
    raw = jnp.clip(jax.random.normal(jax.random.fold_in(base, 4), (TOKENS, width_all)), -5.0, 5.0)
    field = raw * (0.6 + 1.2 * place)
    return field


def draw_keys(key, part):
    field = key_layout(key)
    return field.astype(jnp.bfloat16)


def draw_queries(key, part):
    own = jax.random.fold_in(key, 21)
    raw = jnp.clip(jax.random.normal(own, (TOKENS, HEADS * HEAD_DIM)), -5.0, 5.0)
    return raw.astype(jnp.bfloat16)


def draw_proj_weight(key, part):
    own = jax.random.fold_in(key, 33)
    spread = 0.5 / math.sqrt(HEAD_DIM)
    weight = jnp.clip(jax.random.normal(own, (HEADS, HEAD_DIM, RANK)), -5.0, 5.0) * spread
    return weight.astype(jnp.bfloat16)


def shard_levels(key, shape, shards, smallest, high):
    def one(axis_at, parts):
        draws = jax.random.uniform(jax.random.fold_in(jax.random.fold_in(key, 6), axis_at), (parts,), jnp.float32, smallest / len(shards), high / len(shards))
        return jnp.repeat(jnp.exp(draws), shape[axis_at] // parts).reshape((-1,) + (1,) * (len(shape) - axis_at - 1))

    factor_of = one(*shards[0])
    for cut in shards[1:]:
        factor_of = factor_of * one(*cut)
    return factor_of


def noise(rng, shape, scale, limit, split=(), kind=jnp.bfloat16):
    values = jax.random.normal(rng, shape, jnp.float32) * scale
    if len(split) > 0:
        values = shard_levels(rng, shape, split, -0.22, 0.18) * values
    return jnp.clip(values, min=-limit, max=limit).astype(kind)


def setup_inputs(seed: int = 0) -> dict:
    key_of = jax.random.split(jax.random.key(seed), 6)
    return {
        "queries": draw_queries(jax.random.fold_in(key_of[5], 71), 0),
        "keys": draw_keys(jax.random.fold_in(key_of[5], 71), 0),
        "values": noise(key_of[2], (TOKENS, HEADS * HEAD_DIM), 1.0, 6.0, ((0, 32),)),
        "grad_out": noise(key_of[3], (TOKENS, HEADS * HEAD_DIM), 1.0, 6.0, ((0, 32),)),
        "proj_weight": draw_proj_weight(jax.random.fold_in(key_of[5], 71), 0),
    }


def head_backward(head_args):
    query, key_rows, value_rows, grad_rows, weight = head_args
    seq_len = query.shape[0]
    head_size = query.shape[1]
    score_scale = head_size ** -0.5
    margin = SEG // 2
    seg_count = seq_len // SEG
    logits = jnp.dot(key_rows, weight, preferred_element_type=jnp.float32)
    column_max = jnp.max(logits, axis=0)
    exponent = jnp.exp(logits - column_max[None, :])
    column_sum = jnp.sum(exponent, axis=0)
    exponent_b = exponent.astype(jnp.bfloat16)
    inverse = 1.0 / column_sum
    kbar_f = jnp.dot(exponent_b.T, key_rows, preferred_element_type=jnp.float32) * inverse[:, None]
    vbar_f = jnp.dot(exponent_b.T, value_rows, preferred_element_type=jnp.float32) * inverse[:, None]
    kbar = kbar_f.astype(jnp.bfloat16)
    vbar = vbar_f.astype(jnp.bfloat16)

    def blocks(field):
        padded = jnp.pad(field, ((margin, margin), (0, 0)))
        pieces = padded.reshape(seg_count + 1, SEG, head_size)
        return jnp.concatenate([pieces[:-1], pieces[1:]], axis=1).astype(jnp.float32)

    key_blocks = blocks(key_rows)
    value_blocks = blocks(value_rows)
    key_pos = jnp.arange(seg_count, dtype=jnp.int32)[:, None] * SEG - margin + jnp.arange(2 * SEG, dtype=jnp.int32)[None, :]
    inside_seq = (key_pos >= 0) & (key_pos < seq_len)
    query_segs = query.reshape(seg_count, SEG, head_size).astype(jnp.float32)
    grad_segs = grad_rows.reshape(seg_count, SEG, head_size).astype(jnp.float32)
    kbar32 = kbar.astype(jnp.float32)
    vbar32 = vbar.astype(jnp.float32)
    comp_scores = jnp.einsum("sad,rd->sar", query_segs, kbar32) * score_scale
    window_scores = jnp.einsum("sad,sbd->sab", query_segs, key_blocks) * score_scale
    window_scores = jnp.where(inside_seq[:, None, :], window_scores, -1e30)
    row_max = jnp.maximum(jnp.max(comp_scores, axis=-1), jnp.max(window_scores, axis=-1))
    exp_comp = jnp.exp(comp_scores - row_max[..., None])
    exp_wind = jnp.where(inside_seq[:, None, :], jnp.exp(window_scores - row_max[..., None]), 0.0)
    total = jnp.sum(exp_comp, axis=-1) + jnp.sum(exp_wind, axis=-1)
    prob_comp = exp_comp / total[..., None]
    prob_wind = exp_wind / total[..., None]
    prob_comp_b = prob_comp.astype(jnp.bfloat16).astype(jnp.float32)
    prob_wind_b = prob_wind.astype(jnp.bfloat16).astype(jnp.float32)
    attended = jnp.einsum("sar,rd->sad", prob_comp_b, vbar32) + jnp.einsum("sab,sbd->sad", prob_wind_b, value_blocks)
    row_dot = jnp.sum(grad_segs * attended, axis=-1)
    dprob_comp = (prob_comp * (jnp.einsum("sad,rd->sar", grad_segs, vbar32) - row_dot[..., None])).astype(jnp.bfloat16).astype(jnp.float32)
    dprob_wind = (prob_wind * (jnp.einsum("sad,sbd->sab", grad_segs, value_blocks) - row_dot[..., None])).astype(jnp.bfloat16).astype(jnp.float32)
    grad_query = score_scale * (jnp.einsum("sar,rd->sad", dprob_comp, kbar32) + jnp.einsum("sab,sbd->sad", dprob_wind, key_blocks))
    grad_query = grad_query.reshape(seq_len, head_size).astype(jnp.bfloat16)
    dkbar = (score_scale * jnp.einsum("sar,sad->rd", dprob_comp, query_segs)).astype(jnp.bfloat16)
    dvbar = jnp.einsum("sar,sad->rd", prob_comp_b, grad_segs).astype(jnp.bfloat16)
    dkey_blocks = score_scale * jnp.einsum("sab,sad->sbd", dprob_wind, query_segs)
    dvalue_blocks = jnp.einsum("sab,sad->sbd", prob_wind_b, grad_segs)

    def unblock(field):
        zero_piece = jnp.zeros((1, SEG, head_size), jnp.float32)
        pieces = jnp.concatenate([field[:, :SEG], zero_piece], axis=0) + jnp.concatenate([zero_piece, field[:, SEG:]], axis=0)
        return pieces.reshape((seg_count + 1) * SEG, head_size)[margin:margin + seq_len]

    wgrad_k = unblock(dkey_blocks)
    wgrad_v = unblock(dvalue_blocks)
    column_prob = exponent_b.astype(jnp.float32) * inverse[None, :]
    column_prob_b = column_prob.astype(jnp.bfloat16)
    dprob = jnp.dot(key_rows, dkbar.T, preferred_element_type=jnp.float32) + jnp.dot(value_rows, dvbar.T, preferred_element_type=jnp.float32)
    column_dot = jnp.sum(column_prob * dprob, axis=0)
    logit_grad = (column_prob * (dprob - column_dot[None, :])).astype(jnp.bfloat16)
    grad_key = wgrad_k + jnp.dot(column_prob_b, dkbar, preferred_element_type=jnp.float32) + jnp.dot(logit_grad, weight.T, preferred_element_type=jnp.float32)
    grad_value = wgrad_v + jnp.dot(column_prob_b, dvbar, preferred_element_type=jnp.float32)
    grad_weight = jnp.dot(key_rows.T, logit_grad, preferred_element_type=jnp.float32)
    return grad_query, grad_key.astype(jnp.bfloat16), grad_value.astype(jnp.bfloat16), grad_weight


def reference(queries, keys, values, grad_out, proj_weight):
    def split_heads(field):
        return jnp.transpose(field.reshape(TOKENS, HEADS, HEAD_DIM), (1, 0, 2))

    grad_q, grad_k, grad_v, grad_w = lax.map(head_backward, (split_heads(queries), split_heads(keys), split_heads(values), split_heads(grad_out), proj_weight))

    def join_heads(field):
        return jnp.transpose(field, (1, 0, 2)).reshape(TOKENS, HEADS * HEAD_DIM)

    return join_heads(grad_q), join_heads(grad_k), join_heads(grad_v), grad_w.reshape(HEADS * HEAD_DIM, RANK)
```

```python
import math

import jax
import jax.numpy as jnp
from jax import lax
from jax.experimental import pallas as pl
from jax.experimental.pallas import tpu as pltpu
from jax.sharding import PartitionSpec as P

SEG = 256
STAT_ROWS = 8
DOT_ROWS = 16
BF = jnp.bfloat16
FL = jnp.float32


def dot_nn(a, b):
    return lax.dot_general(a, b, (((1,), (0,)), ((), ())), preferred_element_type=FL)


def dot_nt(a, b):
    return lax.dot_general(a, b, (((1,), (1,)), ((), ())), preferred_element_type=FL)


def dot_tn(a, b):
    return lax.dot_general(a, b, (((0,), (0,)), ((), ())), preferred_element_type=FL)


def struct(shape, dtype):
    return jax.ShapeDtypeStruct(shape, dtype)


def full_spec(shape):
    return pl.BlockSpec(shape, lambda i, pos: (0,) * len(shape))


def call(kernel, name, pos, ins, outs, scratch=(), specs=None):
    specs = specs or {}
    in_specs = [specs[i] if i in specs else full_spec(x.shape) for i, x in enumerate(ins)]
    grid_spec = pltpu.PrefetchScalarGridSpec(
        num_scalar_prefetch=1,
        grid=(1,),
        in_specs=in_specs,
        out_specs=[full_spec(o.shape) for o in outs],
        scratch_shapes=list(scratch),
    )
    return pl.pallas_call(kernel, grid_spec=grid_spec, out_shape=list(outs), name=name)(pos, *ins)


class Plan:
    def __init__(self, devices, tokens_here, head_count, head_size, rank):
        self.inner = math.gcd(max(head_count // 2, 1), devices)
        self.outer = devices // self.inner
        self.heads = head_count // self.inner
        self.devices = devices
        self.tokens = tokens_here
        self.group = tokens_here * self.inner
        self.head_size = head_size
        self.rank = rank
        self.pair = 2 * head_size
        self.width = self.heads * self.pair
        self.rows = self.heads * rank // self.outer
        self.margin = SEG // 2
        self.scale = head_size ** (-0.5)


def pack_kernel(plan, pos, a_ref, b_ref, *outs):
    hd, pair = plan.head_size, plan.pair
    for k, out in enumerate(outs):
        dest = pos[1] ^ k
        for h in range(plan.heads):
            col = pl.multiple_of((dest * plan.heads + h) * hd, hd)
            out[:, h * pair : h * pair + hd] = a_ref[:, pl.ds(col, hd)]
            out[:, h * pair + hd : (h + 1) * pair] = b_ref[:, pl.ds(col, hd)]


def unpack_pair_kernel(plan, pos, *refs):
    ins, (a_ref, b_ref) = refs[: plan.inner], refs[plan.inner :]
    hd, pair = plan.head_size, plan.pair
    for k, src in enumerate(ins):
        dest = pos[1] ^ k
        for h in range(plan.heads):
            col = pl.multiple_of((dest * plan.heads + h) * hd, hd)
            a_ref[:, pl.ds(col, hd)] = src[:, h * pair : h * pair + hd]
            b_ref[:, pl.ds(col, hd)] = src[:, h * pair + hd : (h + 1) * pair]


def unpack_kernel(plan, pos, *refs):
    ins, a_ref = refs[: plan.inner], refs[plan.inner]
    wide = plan.heads * plan.head_size
    for k, src in enumerate(ins):
        col = pl.multiple_of((pos[1] ^ k) * wide, wide)
        a_ref[:, pl.ds(col, wide)] = src[...]


def stats_kernel(plan, pos, *refs):
    pieces, w_ref = refs[: plan.inner], refs[plan.inner]
    kv_ref, first_ref, last_ref = refs[plan.inner + 1 : plan.inner + 4]
    outs = refs[plan.inner + 4 : plan.inner + 4 + plan.outer]
    logit_ref, expo_ref, part_ref = refs[plan.inner + 4 + plan.outer :]
    hd, pair, rank = plan.head_size, plan.pair, plan.rank
    for k, src in enumerate(pieces):
        row = pl.multiple_of((pos[1] ^ k) * plan.tokens, plan.tokens)
        kv_ref[pl.ds(row, plan.tokens), :] = src[...]
    first_ref[...] = kv_ref[: plan.margin, :]
    last_ref[...] = kv_ref[plan.group - plan.margin :, :]
    steps = plan.group // SEG
    tops, sums = [], []
    for h in range(plan.heads):

        def logits_step(i, top):
            at = pl.multiple_of(i * SEG, SEG)
            block = dot_nn(kv_ref[pl.ds(at, SEG), h * pair : h * pair + hd], w_ref[h])
            logit_ref[pl.ds(at, SEG), :] = block
            return jnp.maximum(top, jnp.max(block.reshape(SEG // 8, 8, rank), axis=0))

        top = lax.fori_loop(0, steps, logits_step, jnp.full((8, rank), -jnp.inf, FL))
        top = jnp.max(top, axis=0, keepdims=True)

        def expo_step(i, total):
            at = pl.multiple_of(i * SEG, SEG)
            block = jnp.exp(logit_ref[pl.ds(at, SEG), :] - top)
            expo_ref[pl.ds(at, SEG), :] = block.astype(BF)
            return total + jnp.sum(block.reshape(SEG // 8, 8, rank), axis=0)

        total = lax.fori_loop(0, steps, expo_step, jnp.zeros((8, rank), FL))
        total = jnp.sum(total, axis=0, keepdims=True)
        part_ref[h * rank : (h + 1) * rank, :] = dot_tn(
            expo_ref[...], kv_ref[:, h * pair : (h + 1) * pair]
        )
        tops.append(top)
        sums.append(total)
    pad = jnp.zeros((STAT_ROWS - 2 * plan.heads, rank), FL)
    stats = jnp.concatenate(tops + sums + [pad], axis=0)
    for k, out in enumerate(outs):
        row = pl.multiple_of((pos[0] ^ k) * plan.rows, plan.rows)
        out[: plan.rows, :] = part_ref[pl.ds(row, plan.rows), :]
        out[plan.rows :, :] = stats


def own_columns(plan, pos, wide):
    start = (pos[0] * plan.rows) % plan.rank
    row_at = lax.broadcasted_iota(jnp.int32, (plan.rows, wide), 0)
    col_at = lax.broadcasted_iota(jnp.int32, (plan.rows, wide), 1)
    return col_at == row_at + start


def combine_kernel(plan, pos, *refs):
    ins = refs[: plan.outer]
    full_ref, half_ref, stat_ref = refs[plan.outer :]
    heads, rows = plan.heads, plan.rows
    stats = [r[rows:, :] for r in ins]
    tops = [s[:heads, :] for s in stats]
    top = tops[0]
    for t in tops[1:]:
        top = jnp.maximum(top, t)
    weights = [jnp.exp(t - top) for t in tops]
    total = weights[0] * stats[0][heads : 2 * heads, :]
    for w, s in zip(weights[1:], stats[1:]):
        total = total + w * s[heads : 2 * heads, :]
    inverse = 1.0 / total
    stat_ref[:heads, :] = top
    stat_ref[heads : 2 * heads, :] = inverse
    stat_ref[2 * heads :, :] = jnp.zeros((STAT_ROWS - 2 * heads, plan.rank), FL)
    own = own_columns(plan, pos, plan.rank)
    head_at = (pos[0] * rows) // plan.rank

    def column(field):
        row = field[:1, :]
        for h in range(1, heads):
            row = jnp.where(head_at == h, field[h : h + 1, :], row)
        return jnp.sum(jnp.where(own, row, 0.0), axis=1, keepdims=True)

    result = ins[0][:rows, :] * column(weights[0])
    for w, r in zip(weights[1:], ins[1:]):
        result = result + r[:rows, :] * column(w)
    result = result * column(inverse)
    full_ref[...] = result
    half_ref[...] = result.astype(BF)


def attend_kernel(plan, total_groups, pos, *refs):
    outer, inner, heads = plan.outer, plan.inner, plan.heads
    kv_ref, before_ref, after_ref = refs[:3]
    bars = refs[3 : 3 + outer]
    qg = refs[3 + outer : 3 + outer + inner]
    at = 3 + outer + inner
    dq_outs = refs[at : at + inner]
    bar_outs = refs[at + inner : at + inner + outer]
    wg_ref, wg_before_ref, wg_after_ref = refs[at + inner + outer : at + inner + outer + 3]
    ext_ref, bar_ref, q_ref, acc_ref, dbar_ref, dq_ref, key_ref, val_ref, s_ref = refs[
        at + inner + outer + 3 :
    ]
    hd, pair, rank, margin, group = plan.head_size, plan.pair, plan.rank, plan.margin, plan.group
    ext_ref[:margin, :] = before_ref[...]
    ext_ref[margin : margin + group, :] = kv_ref[...]
    ext_ref[margin + group :, :] = after_ref[...]
    for k, src in enumerate(bars):
        row = pl.multiple_of((pos[0] ^ k) * plan.rows, plan.rows)
        bar_ref[pl.ds(row, plan.rows), :] = src[...]
    for k, src in enumerate(qg):
        row = pl.multiple_of((pos[1] ^ k) * plan.tokens, plan.tokens)
        q_ref[pl.ds(row, plan.tokens), :] = src[...]
    acc_ref[...] = jnp.zeros(acc_ref.shape, FL)
    dbar_ref[...] = jnp.zeros(dbar_ref.shape, FL)
    segs = group // SEG
    at_start = pos[0] == 0
    at_end = pos[0] == total_groups - 1
    for h in range(heads):
        low = h * pair
        mid = low + hd
        high = low + pair
        key_ref[:rank, :] = bar_ref[h * rank : (h + 1) * rank, :hd]
        val_ref[:rank, :] = bar_ref[h * rank : (h + 1) * rank, hd:]

        def step(j, carry):
            row = pl.multiple_of(j * SEG, SEG)
            key_ref[rank:, :] = ext_ref[pl.ds(row, 2 * SEG), low:mid]
            val_ref[rank:, :] = ext_ref[pl.ds(row, 2 * SEG), mid:high]
            query = q_ref[pl.ds(row, SEG), low:mid]
            grad = q_ref[pl.ds(row, SEG), mid:high]
            s_ref[...] = dot_nt(key_ref[...], query) * plan.scale

            @pl.when(jnp.logical_and(at_start, j == 0))
            def _():
                s_ref[rank : rank + margin, :] = jnp.full((margin, SEG), -1e30, FL)

            @pl.when(jnp.logical_and(at_end, j == segs - 1))
            def _():
                s_ref[rank + 2 * SEG - margin :, :] = jnp.full((margin, SEG), -1e30, FL)

            scores = s_ref[...]
            expo = jnp.exp(scores - jnp.max(scores, axis=0, keepdims=True))
            prob = expo * (1.0 / jnp.sum(expo, axis=0, keepdims=True))
            prob_b = prob.astype(BF)
            dprob = dot_nt(val_ref[...], grad)
            row_dot = jnp.sum(prob_b.astype(FL) * dprob, axis=0, keepdims=True)
            dscore = (prob * (dprob - row_dot)).astype(BF)
            dquery = dot_tn(key_ref[...], dscore) * plan.scale
            dq_ref[pl.ds(row, SEG), h * hd : (h + 1) * hd] = jnp.transpose(dquery).astype(BF)
            dkey = dot_nn(dscore, query) * plan.scale
            dval = dot_nn(prob_b, grad)
            dbar_ref[h * rank : (h + 1) * rank, :hd] += dkey[:rank, :]
            dbar_ref[h * rank : (h + 1) * rank, hd:] += dval[:rank, :]
            acc_ref[pl.ds(row, 2 * SEG), low:mid] += dkey[rank:, :]
            acc_ref[pl.ds(row, 2 * SEG), mid:high] += dval[rank:, :]
            return carry

        lax.fori_loop(0, segs, step, 0)
    for k, out in enumerate(dq_outs):
        row = pl.multiple_of((pos[1] ^ k) * plan.tokens, plan.tokens)
        out[...] = dq_ref[pl.ds(row, plan.tokens), :]
    for k, out in enumerate(bar_outs):
        row = pl.multiple_of((pos[0] ^ k) * plan.rows, plan.rows)
        out[...] = dbar_ref[pl.ds(row, plan.rows), :].astype(BF)
    wg_ref[...] = acc_ref[margin : margin + group, :]
    wg_before_ref[...] = acc_ref[:margin, :].astype(BF)
    wg_after_ref[...] = acc_ref[margin + group :, :].astype(BF)


def combine_grad_kernel(plan, pos, *refs):
    full_ref, ins = refs[0], refs[1 : 1 + plan.outer]
    out_ref = refs[1 + plan.outer]
    total = ins[0][...].astype(FL)
    for r in ins[1:]:
        total = total + r[...].astype(FL)
    half = total.astype(BF)
    out_ref[: plan.rows, :] = half
    column = jnp.sum(full_ref[...] * half.astype(FL), axis=1, keepdims=True)
    own = own_columns(plan, pos, plan.rank)
    rest = jnp.sum(jnp.where(own, column, 0.0), axis=0, keepdims=True)
    parts = []
    for _ in range(3):
        part = rest.astype(BF).astype(FL)
        parts.append(part)
        rest = rest - part
    parts.append(jnp.zeros((DOT_ROWS - 3, plan.rank), FL))
    out_ref[plan.rows :, :] = jnp.concatenate(parts, axis=0).astype(BF)


def finish_kernel(plan, pos, *refs):
    outer, inner, heads = plan.outer, plan.inner, plan.heads
    kv_ref, w_ref, stat_ref, wg_ref, before_ref, after_ref = refs[:6]
    bars = refs[6 : 6 + outer]
    at = 6 + outer
    outs = refs[at : at + inner]
    proj_outs = refs[at + inner : at + inner + outer]
    bar_ref, grad_ref, sum_ref, proj_ref = refs[at + inner + outer :]
    hd, pair, rank, margin, group = plan.head_size, plan.pair, plan.rank, plan.margin, plan.group
    dots = []
    for k, src in enumerate(bars):
        row = pl.multiple_of((pos[0] ^ k) * plan.rows, plan.rows)
        bar_ref[pl.ds(row, plan.rows), :] = src[: plan.rows, :]
        dots.append(jnp.sum(src[plan.rows :, :].astype(FL), axis=0, keepdims=True))
    proj_ref[...] = jnp.zeros(proj_ref.shape, FL)
    segs = group // SEG
    for h in range(heads):
        low, high = h * pair, (h + 1) * pair
        column_dot = jnp.zeros((1, rank), FL)
        for k, d in enumerate(dots):
            here = ((pos[0] ^ k) * plan.rows) // rank == h
            column_dot = column_dot + jnp.where(here, d, 0.0)
        top = stat_ref[h : h + 1, :]
        inverse = stat_ref[heads + h : heads + h + 1, :]

        def step(i, carry):
            row = pl.multiple_of(i * SEG, SEG)
            both = kv_ref[pl.ds(row, SEG), low:high]
            key = both[:, :hd]
            dbar = bar_ref[h * rank : (h + 1) * rank, :]
            expo = jnp.exp(dot_nn(key, w_ref[h]) - top).astype(BF).astype(FL)
            prob = expo * inverse
            dprob = dot_nt(both, dbar)
            logit_grad = (prob * (dprob - column_dot)).astype(BF)
            sum_ref[...] = dot_nn(prob.astype(BF), dbar) + wg_ref[pl.ds(row, SEG), low:high]
            sum_ref[:, :hd] += dot_nt(logit_grad, w_ref[h])

            @pl.when(i == 0)
            def _():
                sum_ref[:margin, :] += before_ref[:, low:high].astype(FL)

            @pl.when(i == segs - 1)
            def _():
                sum_ref[SEG - margin :, :] += after_ref[:, low:high].astype(FL)

            grad_ref[pl.ds(row, SEG), low:high] = sum_ref[...].astype(BF)
            proj_ref[h * hd : (h + 1) * hd, :] += dot_tn(key, logit_grad)
            return carry

        lax.fori_loop(0, segs, step, 0)
    for k, out in enumerate(outs):
        row = pl.multiple_of((pos[1] ^ k) * plan.tokens, plan.tokens)
        out[...] = grad_ref[pl.ds(row, plan.tokens), :]
    piece = plan.heads * hd // outer
    for k, out in enumerate(proj_outs):
        row = pl.multiple_of((pos[0] ^ k) * piece, piece)
        out[...] = proj_ref[pl.ds(row, piece), :]


def exchange(fields, devices, stride):
    out = [fields[0]]
    for k in range(1, len(fields)):
        flip = [(i, i ^ (k * stride)) for i in range(devices)]
        out.append(lax.ppermute(fields[k], "seq", flip))
    return out


def per_device(queries, keys, values, grad_out, proj_weight):
    tokens_here, row_width = queries.shape
    head_count, head_size, rank = proj_weight.shape
    devices = lax.axis_size("seq")
    plan = Plan(devices, tokens_here, head_count, head_size, rank)
    inner, outer, heads = plan.inner, plan.outer, plan.heads
    group, width, rows, margin = plan.group, plan.width, plan.rows, plan.margin
    me = lax.axis_index("seq")
    pos = jnp.stack([me // inner, me % inner]).astype(jnp.int32)

    def bind(kernel, *more):
        return lambda pos_ref, *refs: kernel(plan, *more, pos_ref, *refs)

    w_spec = pl.BlockSpec((heads, head_size, rank), lambda i, p: (p[1], 0, 0))
    wide_piece = struct((tokens_here, width), BF)
    kv_send = call(bind(pack_kernel), "pack_kv", pos, [keys, values], [wide_piece] * inner)
    kv_pieces = exchange(kv_send, devices, 1)
    *kv_pieces, queries, grad_out = lax.optimization_barrier((*kv_pieces, queries, grad_out))
    qg_send = call(bind(pack_kernel), "pack_qg", pos, [queries, grad_out], [wide_piece] * inner)
    qg_pieces = exchange(qg_send, devices, 1)

    stat_piece = struct((rows + STAT_ROWS, rank), FL)
    kv_all, kv_first, kv_last, *part_send = call(
        bind(stats_kernel),
        "stats",
        pos,
        [*kv_pieces, proj_weight],
        [struct((group, width), BF), struct((margin, width), BF), struct((margin, width), BF)]
        + [stat_piece] * outer,
        [
            pltpu.VMEM((group, rank), FL),
            pltpu.VMEM((group, rank), BF),
            pltpu.VMEM((heads * rank, plan.pair), FL),
        ],
        {inner: w_spec},
    )
    parts = exchange(part_send, devices, inner)
    up = [(i, i + inner) for i in range(devices - inner)]
    down = [(j, i) for i, j in up]
    kv_before = lax.ppermute(kv_last, "seq", up)
    kv_after = lax.ppermute(kv_first, "seq", down)
    bar_full, bar_half, stats = call(
        bind(combine_kernel),
        "combine",
        pos,
        parts,
        [struct((rows, plan.pair), FL), struct((rows, plan.pair), BF), struct((STAT_ROWS, rank), FL)],
    )
    bars = exchange([bar_half] * outer, devices, inner)

    dq_piece = struct((tokens_here, heads * head_size), BF)
    edge = struct((margin, width), BF)
    results = call(
        bind(attend_kernel, outer),
        "attend",
        pos,
        [kv_all, kv_before, kv_after, *bars, *qg_pieces],
        [dq_piece] * inner
        + [struct((rows, plan.pair), BF)] * outer
        + [struct((group, width), FL), edge, edge],
        [
            pltpu.VMEM((group + 2 * margin, width), BF),
            pltpu.VMEM((heads * rank, plan.pair), BF),
            pltpu.VMEM((group, width), BF),
            pltpu.VMEM((group + 2 * margin, width), FL),
            pltpu.VMEM((heads * rank, plan.pair), FL),
            pltpu.VMEM((group, heads * head_size), BF),
            pltpu.VMEM((rank + 2 * SEG, head_size), BF),
            pltpu.VMEM((rank + 2 * SEG, head_size), BF),
            pltpu.VMEM((rank + 2 * SEG, SEG), FL),
        ],
    )
    dq_send = results[:inner]
    dbar_send = results[inner : inner + outer]
    wg, wg_before, wg_after = results[inner + outer :]
    dbar_parts = exchange(dbar_send, devices, inner)
    wg_from_after = lax.ppermute(wg_before, "seq", down)
    wg_from_before = lax.ppermute(wg_after, "seq", up)
    (dbar_half,) = call(
        bind(combine_grad_kernel),
        "combine_grad",
        pos,
        [bar_full, *dbar_parts],
        [struct((rows + DOT_ROWS, plan.pair), BF)],
    )
    dbars = exchange([dbar_half] * outer, devices, inner)
    dq_pieces = exchange(dq_send, devices, 1)

    proj_piece = struct((heads * head_size // outer, rank), FL)
    results = call(
        bind(finish_kernel),
        "finish",
        pos,
        [kv_all, proj_weight, stats, wg, wg_from_before, wg_from_after, *dbars],
        [wide_piece] * inner + [proj_piece] * outer,
        [
            pltpu.VMEM((heads * rank, plan.pair), BF),
            pltpu.VMEM((group, width), BF),
            pltpu.VMEM((SEG, plan.pair), FL),
            pltpu.VMEM((heads * head_size, rank), FL),
        ],
        {1: w_spec},
    )
    dkv_pieces = exchange(results[:inner], devices, 1)
    proj_parts = exchange(results[inner:], devices, inner)
    whole = struct((tokens_here, row_width), BF)
    (grad_queries,) = call(bind(unpack_kernel), "unpack_q", pos, dq_pieces, [whole])
    proj_sum = proj_parts[0]
    for part in proj_parts[1:]:
        proj_sum = proj_sum + part
    place = [(o * inner + p, p * outer + o) for o in range(outer) for p in range(inner)]
    grad_proj = lax.ppermute(proj_sum, "seq", place)
    grad_keys, grad_values = call(
        bind(unpack_pair_kernel), "unpack_kv", pos, dkv_pieces, [whole, whole]
    )
    return (grad_queries, grad_keys, grad_values, grad_proj)


def solution(mesh):
    in_specs = (P("seq", None), P("seq", None), P("seq", None), P("seq", None), P())
    out_specs = (P("seq", None), P("seq", None), P("seq", None), P("seq", None))
    return jax.shard_map(
        per_device, mesh=mesh, in_specs=in_specs, out_specs=out_specs, check_vma=False
    )
```

```python
import math

import jax
import jax.numpy as jnp
from jax import lax
from jax.experimental import pallas as pl
from jax.experimental.pallas import tpu as pltpu
from jax.sharding import PartitionSpec as P


SEG = 256
STAT_ROWS = 8
DOT_ROWS = 16
HIDDEN = -1e30
BF = jnp.bfloat16
FL = jnp.float32


def dot_nn(a, b):
    return lax.dot_general(a, b, (((1,), (0,)), ((), ())), preferred_element_type=FL)


def dot_nt(a, b):
    return lax.dot_general(a, b, (((1,), (1,)), ((), ())), preferred_element_type=FL)


def dot_tn(a, b):
    return lax.dot_general(a, b, (((0,), (0,)), ((), ())), preferred_element_type=FL)


def struct(shape, dtype):
    return jax.ShapeDtypeStruct(shape, dtype)


def size_of(x):
    dtype = jnp.dtype(x.dtype)
    return math.prod(x.shape) * dtype.itemsize


def call(kernel, pos, ins, outs, scratch=(), spare=4):
    on_chip = pl.BlockSpec(memory_space=pltpu.VMEM)
    need = sum(size_of(x) for x in (*ins, *outs, *scratch))
    return pl.pallas_call(
        kernel,
        in_specs=[pl.BlockSpec(memory_space=pltpu.SMEM)] + [on_chip] * len(ins),
        out_specs=[on_chip] * len(outs),
        out_shape=list(outs),
        scratch_shapes=list(scratch),
        compiler_params=pltpu.CompilerParams(vmem_limit_bytes=need + spare * 2**20),
    )(pos, *ins)


class Plan:
    def __init__(self, devices, tokens_here, head_count, head_size, rank):
        self.inner = math.gcd(max(head_count // 2, 1), devices)
        self.outer = devices // self.inner
        self.heads = head_count // self.inner
        self.tokens = tokens_here
        self.group = tokens_here * self.inner
        self.head_size = head_size
        self.rank = rank
        self.pair = 2 * head_size
        self.width = self.heads * self.pair
        self.rows = self.heads * rank // self.outer
        self.margin = SEG // 2
        self.scale = head_size ** (-0.5)


def pack_kernel(plan, pos, a_ref, b_ref, *outs):
    hd, pair = plan.head_size, plan.pair
    for k, out in enumerate(outs):
        dest = pos[1] ^ k
        for h in range(plan.heads):
            col = pl.multiple_of((dest * plan.heads + h) * hd, hd)
            out[:, h * pair : h * pair + hd] = a_ref[:, pl.ds(col, hd)]
            out[:, h * pair + hd : (h + 1) * pair] = b_ref[:, pl.ds(col, hd)]


def unpack_pair_kernel(plan, pos, *refs):
    ins, (a_ref, b_ref) = refs[: plan.inner], refs[plan.inner :]
    hd, pair = plan.head_size, plan.pair
    for k, src in enumerate(ins):
        dest = pos[1] ^ k
        for h in range(plan.heads):
            col = pl.multiple_of((dest * plan.heads + h) * hd, hd)
            a_ref[:, pl.ds(col, hd)] = src[:, h * pair : h * pair + hd]
            b_ref[:, pl.ds(col, hd)] = src[:, h * pair + hd : (h + 1) * pair]


def unpack_kernel(plan, pos, *refs):
    ins, a_ref = refs[: plan.inner], refs[plan.inner]
    wide = plan.heads * plan.head_size
    for k, src in enumerate(ins):
        col = pl.multiple_of((pos[1] ^ k) * wide, wide)
        a_ref[:, pl.ds(col, wide)] = src[...]


def stats_kernel(plan, pos, *refs):
    pieces, w_ref = refs[: plan.inner], refs[plan.inner]
    kv_ref, first_ref, last_ref = refs[plan.inner + 1 : plan.inner + 4]
    outs = refs[plan.inner + 4 : plan.inner + 4 + plan.outer]
    logit_ref, expo_ref, part_ref = refs[plan.inner + 4 + plan.outer :]
    hd, pair, rank = plan.head_size, plan.pair, plan.rank
    for k, src in enumerate(pieces):
        row = pl.multiple_of((pos[1] ^ k) * plan.tokens, plan.tokens)
        kv_ref[pl.ds(row, plan.tokens), :] = src[...]
    first_ref[...] = kv_ref[: plan.margin, :]
    last_ref[...] = kv_ref[plan.group - plan.margin :, :]
    steps = plan.group // SEG
    tops, sums = [], []
    for h in range(plan.heads):

        def logits_step(i, top):
            at = pl.multiple_of(i * SEG, SEG)
            block = dot_nn(kv_ref[pl.ds(at, SEG), h * pair : h * pair + hd], w_ref[h])
            logit_ref[pl.ds(at, SEG), :] = block
            return jnp.maximum(top, jnp.max(block.reshape(SEG // 8, 8, rank), axis=0))

        top = lax.fori_loop(0, steps, logits_step, jnp.full((8, rank), -jnp.inf, FL))
        top = jnp.max(top, axis=0, keepdims=True)

        def expo_step(i, total):
            at = pl.multiple_of(i * SEG, SEG)
            block = jnp.exp(logit_ref[pl.ds(at, SEG), :] - top)
            expo_ref[pl.ds(at, SEG), :] = block.astype(BF)
            return total + jnp.sum(block.reshape(SEG // 8, 8, rank), axis=0)

        total = lax.fori_loop(0, steps, expo_step, jnp.zeros((8, rank), FL))
        total = jnp.sum(total, axis=0, keepdims=True)
        part_ref[h * rank : (h + 1) * rank, :] = dot_tn(
            expo_ref[...], kv_ref[:, h * pair : (h + 1) * pair]
        )
        tops.append(top)
        sums.append(total)
    pad = jnp.zeros((STAT_ROWS - 2 * plan.heads, rank), FL)
    stats = jnp.concatenate(tops + sums + [pad], axis=0)
    for k, out in enumerate(outs):
        row = pl.multiple_of((pos[0] ^ k) * plan.rows, plan.rows)
        out[: plan.rows, :] = part_ref[pl.ds(row, plan.rows), :]
        out[plan.rows :, :] = stats


def own_columns(plan, pos, wide):
    start = (pos[0] * plan.rows) % plan.rank
    row_at = lax.broadcasted_iota(jnp.int32, (plan.rows, wide), 0)
    col_at = lax.broadcasted_iota(jnp.int32, (plan.rows, wide), 1)
    return col_at == row_at + start


def combine_kernel(plan, pos, *refs):
    ins = refs[: plan.outer]
    full_ref, half_ref, stat_ref = refs[plan.outer :]
    heads, rows = plan.heads, plan.rows
    stats = [r[rows:, :] for r in ins]
    tops = [s[:heads, :] for s in stats]
    top = tops[0]
    for t in tops[1:]:
        top = jnp.maximum(top, t)
    weights = [jnp.exp(t - top) for t in tops]
    total = weights[0] * stats[0][heads : 2 * heads, :]
    for w, s in zip(weights[1:], stats[1:]):
        total = total + w * s[heads : 2 * heads, :]
    inverse = 1.0 / total
    stat_ref[:heads, :] = top
    stat_ref[heads : 2 * heads, :] = inverse
    stat_ref[2 * heads :, :] = jnp.zeros((STAT_ROWS - 2 * heads, plan.rank), FL)
    own = own_columns(plan, pos, plan.rank)
    head_at = (pos[0] * rows) // plan.rank

    def column(field):
        row = field[:1, :]
        for h in range(1, heads):
            row = jnp.where(head_at == h, field[h : h + 1, :], row)
        return jnp.sum(jnp.where(own, row, 0.0), axis=1, keepdims=True)

    result = ins[0][:rows, :] * column(weights[0])
    for w, r in zip(weights[1:], ins[1:]):
        result = result + r[:rows, :] * column(w)
    result = result * column(inverse)
    full_ref[...] = result
    half_ref[...] = result.astype(BF)


def attend_kernel(plan, total_groups, pos, *refs):
    outer, inner, heads = plan.outer, plan.inner, plan.heads
    kv_ref, before_ref, after_ref = refs[:3]
    bars = refs[3 : 3 + outer]
    qg = refs[3 + outer : 3 + outer + inner]
    at = 3 + outer + inner
    dq_outs = refs[at : at + inner]
    bar_outs = refs[at + inner : at + inner + outer]
    wg_ref, wg_before_ref, wg_after_ref = refs[at + inner + outer : at + inner + outer + 3]
    ext_ref, bar_ref, q_ref, acc_ref, dbar_ref, dq_ref = refs[
        at + inner + outer + 3 :
    ]
    hd, pair, rank, margin, group = plan.head_size, plan.pair, plan.rank, plan.margin, plan.group
    ext_ref[:margin, :] = before_ref[...]
    ext_ref[margin : margin + group, :] = kv_ref[...]
    ext_ref[margin + group :, :] = after_ref[...]
    for k, src in enumerate(bars):
        row = pl.multiple_of((pos[0] ^ k) * plan.rows, plan.rows)
        bar_ref[pl.ds(row, plan.rows), :] = src[...]
    for k, src in enumerate(qg):
        row = pl.multiple_of((pos[1] ^ k) * plan.tokens, plan.tokens)
        q_ref[pl.ds(row, plan.tokens), :] = src[...]
    acc_ref[...] = jnp.zeros(acc_ref.shape, FL)
    dbar_ref[...] = jnp.zeros(dbar_ref.shape, FL)
    segs = group // SEG
    at_start = pos[0] == 0
    at_end = pos[0] == total_groups - 1
    factor = plan.scale / math.log(2.0)

    def step(j, carry):
        row = pl.multiple_of(j * SEG, SEG)
        hide_low = jnp.where(jnp.logical_and(at_start, j == 0), HIDDEN, 0.0)
        hide_high = jnp.where(jnp.logical_and(at_end, j == segs - 1), HIDDEN, 0.0)
        loaded, scored = [], []
        for h in range(heads):
            low, mid, high = h * pair, h * pair + hd, (h + 1) * pair
            bar = slice(h * rank, (h + 1) * rank)
            key = jnp.concatenate([bar_ref[bar, :hd], ext_ref[pl.ds(row, 2 * SEG), low:mid]], axis=0)
            val = jnp.concatenate([bar_ref[bar, hd:], ext_ref[pl.ds(row, 2 * SEG), mid:high]], axis=0)
            query = q_ref[pl.ds(row, SEG), low:mid]
            grad = q_ref[pl.ds(row, SEG), mid:high]
            loaded.append((key, query, grad))
            scored.append((dot_nt(key, query), dot_nt(val, grad)))
        for h in range(heads):
            low, mid, high = h * pair, h * pair + hd, (h + 1) * pair
            bar = slice(h * rank, (h + 1) * rank)
            key, query, grad = loaded[h]
            scores, dprob = scored[h]
            scores = jnp.concatenate(
                [
                    scores[:rank],
                    scores[rank : rank + margin] + hide_low,
                    scores[rank + margin : rank + 2 * SEG - margin],
                    scores[rank + 2 * SEG - margin :] + hide_high,
                ],
                axis=0,
            )
            expo = jnp.exp2((scores - jnp.max(scores, axis=0, keepdims=True)) * factor)
            prob = expo * (1.0 / jnp.sum(expo, axis=0, keepdims=True))
            prob_b = prob.astype(BF)
            row_dot = jnp.sum(prob_b.astype(FL) * dprob, axis=0, keepdims=True)
            dscore = (prob * (dprob - row_dot)).astype(BF)
            dquery = dot_tn(key, dscore) * plan.scale
            dq_ref[pl.ds(row, SEG), h * hd : (h + 1) * hd] = jnp.transpose(dquery).astype(BF)
            dkey = dot_nn(dscore, query)
            dval = dot_nn(prob_b, grad)
            dbar_ref[bar, :hd] += dkey[:rank, :]
            dbar_ref[bar, hd:] += dval[:rank, :]
            acc_ref[pl.ds(row, 2 * SEG), low:mid] += dkey[rank:, :]
            acc_ref[pl.ds(row, 2 * SEG), mid:high] += dval[rank:, :]
        return carry

    lax.fori_loop(0, segs, step, 0)
    for h in range(heads):
        bar = slice(h * rank, (h + 1) * rank)
        dbar_ref[bar, :hd] = dbar_ref[bar, :hd] * plan.scale
        acc_ref[:, h * pair : h * pair + hd] = acc_ref[:, h * pair : h * pair + hd] * plan.scale
    for k, out in enumerate(dq_outs):
        row = pl.multiple_of((pos[1] ^ k) * plan.tokens, plan.tokens)
        out[...] = dq_ref[pl.ds(row, plan.tokens), :]
    for k, out in enumerate(bar_outs):
        row = pl.multiple_of((pos[0] ^ k) * plan.rows, plan.rows)
        out[...] = dbar_ref[pl.ds(row, plan.rows), :].astype(BF)
    wg_ref[...] = acc_ref[margin : margin + group, :]
    wg_before_ref[...] = acc_ref[:margin, :].astype(BF)
    wg_after_ref[...] = acc_ref[margin + group :, :].astype(BF)


def combine_grad_kernel(plan, pos, *refs):
    full_ref, ins = refs[0], refs[1 : 1 + plan.outer]
    out_ref = refs[1 + plan.outer]
    total = ins[0][...].astype(FL)
    for r in ins[1:]:
        total = total + r[...].astype(FL)
    half = total.astype(BF)
    out_ref[: plan.rows, :] = half
    column = jnp.sum(full_ref[...] * half.astype(FL), axis=1, keepdims=True)
    own = own_columns(plan, pos, plan.rank)
    rest = jnp.sum(jnp.where(own, column, 0.0), axis=0, keepdims=True)
    parts = []
    for _ in range(3):
        part = rest.astype(BF).astype(FL)
        parts.append(part)
        rest = rest - part
    parts.append(jnp.zeros((DOT_ROWS - 3, plan.rank), FL))
    out_ref[plan.rows :, :] = jnp.concatenate(parts, axis=0).astype(BF)


def finish_kernel(plan, pos, *refs):
    outer, inner, heads = plan.outer, plan.inner, plan.heads
    kv_ref, w_ref, stat_ref, wg_ref, before_ref, after_ref = refs[:6]
    bars = refs[6 : 6 + outer]
    at = 6 + outer
    outs = refs[at : at + inner]
    logit_grad_ref, bar_ref, grad_ref, sum_ref = refs[at + inner :]
    hd, pair, rank, margin, group = plan.head_size, plan.pair, plan.rank, plan.margin, plan.group
    dots = []
    for k, src in enumerate(bars):
        row = pl.multiple_of((pos[0] ^ k) * plan.rows, plan.rows)
        bar_ref[pl.ds(row, plan.rows), :] = src[: plan.rows, :]
        dots.append(jnp.sum(src[plan.rows :, :].astype(FL), axis=0, keepdims=True))
    segs = group // SEG
    for h in range(heads):
        low, high = h * pair, (h + 1) * pair
        column_dot = jnp.zeros((1, rank), FL)
        for k, d in enumerate(dots):
            here = ((pos[0] ^ k) * plan.rows) // rank == h
            column_dot = column_dot + jnp.where(here, d, 0.0)
        top = stat_ref[h : h + 1, :]
        inverse = stat_ref[heads + h : heads + h + 1, :]

        def step(i, carry):
            row = pl.multiple_of(i * SEG, SEG)
            both = kv_ref[pl.ds(row, SEG), low:high]
            key = both[:, :hd]
            dbar = bar_ref[h * rank : (h + 1) * rank, :]
            expo = jnp.exp(dot_nn(key, w_ref[h]) - top).astype(BF).astype(FL)
            prob = expo * inverse
            dprob = dot_nt(both, dbar)
            logit_grad = (prob * (dprob - column_dot)).astype(BF)
            sum_ref[...] = dot_nn(prob.astype(BF), dbar) + wg_ref[pl.ds(row, SEG), low:high]
            sum_ref[:, :hd] += dot_nt(logit_grad, w_ref[h])

            @pl.when(i == 0)
            def _():
                sum_ref[:margin, :] += before_ref[:, low:high].astype(FL)

            @pl.when(i == segs - 1)
            def _():
                sum_ref[SEG - margin :, :] += after_ref[:, low:high].astype(FL)

            grad_ref[pl.ds(row, SEG), low:high] = sum_ref[...].astype(BF)
            logit_grad_ref[pl.ds(row, SEG), h * rank : (h + 1) * rank] = logit_grad
            return carry

        lax.fori_loop(0, segs, step, 0)
    for k, out in enumerate(outs):
        row = pl.multiple_of((pos[1] ^ k) * plan.tokens, plan.tokens)
        out[...] = grad_ref[pl.ds(row, plan.tokens), :]


def proj_kernel(plan, pos, kv_ref, logit_grad_ref, *refs):
    outs, proj_ref = refs[: plan.outer], refs[plan.outer]
    hd, pair, rank = plan.head_size, plan.pair, plan.rank
    for h in range(plan.heads):
        proj_ref[h * hd : (h + 1) * hd, :] = dot_tn(
            kv_ref[:, h * pair : h * pair + hd], logit_grad_ref[:, h * rank : (h + 1) * rank]
        )
    piece = plan.heads * hd // plan.outer
    for k, out in enumerate(outs):
        row = pl.multiple_of((pos[0] ^ k) * piece, piece)
        out[...] = proj_ref[pl.ds(row, piece), :]


def exchange(fields, devices, stride):
    out = [fields[0]]
    for k in range(1, len(fields)):
        flip = [(i, i ^ (k * stride)) for i in range(devices)]
        out.append(lax.ppermute(fields[k], "seq", flip))
    return out


def swap_edges(upward, downward, devices, stride):
    up = [(i, i + stride) for i in range(devices - stride)]
    down = [(j, i) for i, j in up]
    return lax.ppermute(upward, "seq", up), lax.ppermute(downward, "seq", down)


def per_device(queries, keys, values, grad_out, proj_weight):
    tokens_here, row_width = queries.shape
    head_count, head_size, rank = proj_weight.shape
    devices = lax.axis_size("seq")
    plan = Plan(devices, tokens_here, head_count, head_size, rank)
    inner, outer, heads = plan.inner, plan.outer, plan.heads
    group, width, rows, margin = plan.group, plan.width, plan.rows, plan.margin
    me = lax.axis_index("seq")
    pos = jnp.stack([me // inner, me % inner]).astype(jnp.int32)

    def bind(kernel, *more):
        return lambda pos_ref, *refs: kernel(plan, *more, pos_ref, *refs)

    weight = lax.dynamic_slice_in_dim(proj_weight, (me % inner) * heads, heads, axis=0)
    wide_piece = struct((tokens_here, width), BF)
    kv_send = call(bind(pack_kernel), pos, [keys, values], [wide_piece] * inner)
    qg_send = call(bind(pack_kernel), pos, [queries, grad_out], [wide_piece] * inner)
    kv_pieces = exchange(kv_send, devices, 1)
    qg_pieces = exchange(qg_send, devices, 1)

    stat_piece = struct((rows + STAT_ROWS, rank), FL)
    kv_all, kv_first, kv_last, *part_send = call(
        bind(stats_kernel),
        pos,
        [*kv_pieces, weight],
        [struct((group, width), BF), struct((margin, width), BF), struct((margin, width), BF)]
        + [stat_piece] * outer,
        [
            pltpu.VMEM((group, rank), FL),
            pltpu.VMEM((group, rank), BF),
            pltpu.VMEM((heads * rank, plan.pair), FL),
        ],
    )
    parts = exchange(part_send, devices, inner)
    kv_before, kv_after = swap_edges(kv_last, kv_first, devices, inner)
    bar_full, bar_half, stats = call(
        bind(combine_kernel),
        pos,
        parts,
        [struct((rows, plan.pair), FL), struct((rows, plan.pair), BF), struct((STAT_ROWS, rank), FL)],
    )
    bars = exchange([bar_half] * outer, devices, inner)

    dq_piece = struct((tokens_here, heads * head_size), BF)
    edge = struct((margin, width), BF)
    results = call(
        bind(attend_kernel, outer),
        pos,
        [kv_all, kv_before, kv_after, *bars, *qg_pieces],
        [dq_piece] * inner
        + [struct((rows, plan.pair), BF)] * outer
        + [struct((group, width), FL), edge, edge],
        [
            pltpu.VMEM((group + 2 * margin, width), BF),
            pltpu.VMEM((heads * rank, plan.pair), BF),
            pltpu.VMEM((group, width), BF),
            pltpu.VMEM((group + 2 * margin, width), FL),
            pltpu.VMEM((heads * rank, plan.pair), FL),
            pltpu.VMEM((group, heads * head_size), BF),
        ],
    )
    dq_send = results[:inner]
    dbar_send = results[inner : inner + outer]
    wg, wg_before, wg_after = results[inner + outer :]
    dbar_parts = exchange(dbar_send, devices, inner)
    wg_from_before, wg_from_after = swap_edges(wg_after, wg_before, devices, inner)
    (dbar_half,) = call(
        bind(combine_grad_kernel),
        pos,
        [bar_full, *dbar_parts],
        [struct((rows + DOT_ROWS, plan.pair), BF)],
    )
    dbars = exchange([dbar_half] * outer, devices, inner)
    dq_pieces = exchange(dq_send, devices, 1)

    proj_piece = struct((heads * head_size // outer, rank), FL)
    results = call(
        bind(finish_kernel),
        pos,
        [kv_all, weight, stats, wg, wg_from_before, wg_from_after, *dbars],
        [wide_piece] * inner + [struct((group, heads * rank), BF)],
        [
            pltpu.VMEM((heads * rank, plan.pair), BF),
            pltpu.VMEM((group, width), BF),
            pltpu.VMEM((SEG, plan.pair), FL),
        ],
    )
    dkv_pieces = exchange(results[:inner], devices, 1)
    proj_send = call(
        bind(proj_kernel),
        pos,
        [kv_all, results[inner]],
        [proj_piece] * outer,
        [pltpu.VMEM((heads * head_size, rank), FL)],
    )
    proj_parts = exchange(proj_send, devices, inner)
    whole = struct((tokens_here, row_width), BF)
    (grad_queries,) = call(bind(unpack_kernel), pos, dq_pieces, [whole])
    proj_sum = proj_parts[0]
    for part in proj_parts[1:]:
        proj_sum = proj_sum + part
    place = [(o * inner + p, p * outer + o) for o in range(outer) for p in range(inner)]
    grad_proj = lax.ppermute(proj_sum, "seq", place)
    grad_keys, grad_values = call(bind(unpack_pair_kernel), pos, dkv_pieces, [whole, whole])
    return (grad_queries, grad_keys, grad_values, grad_proj)


def solution(mesh):
    in_specs = (P("seq", None), P("seq", None), P("seq", None), P("seq", None), P())
    out_specs = (P("seq", None), P("seq", None), P("seq", None), P("seq", None))
    return jax.shard_map(
        per_device, mesh=mesh, in_specs=in_specs, out_specs=out_specs, check_vma=False
    )
```

```python
import math

import jax
import jax.numpy as jnp
from jax import lax
from jax.experimental import pallas as pl
from jax.experimental.pallas import tpu as pltpu
from jax.sharding import PartitionSpec as P


SEG = 256
STAT_ROWS = 8
DOT_ROWS = 16
HIDDEN = -1e30
HEADS_PER_DEVICE = 2
BF = jnp.bfloat16
FL = jnp.float32


def dot_nn(a, b):
    return lax.dot_general(a, b, (((1,), (0,)), ((), ())), preferred_element_type=FL)


def dot_nt(a, b):
    return lax.dot_general(a, b, (((1,), (1,)), ((), ())), preferred_element_type=FL)


def dot_tn(a, b):
    return lax.dot_general(a, b, (((0,), (0,)), ((), ())), preferred_element_type=FL)


def struct(shape, dtype):
    return jax.ShapeDtypeStruct(shape, dtype)


def size_of(x):
    dtype = jnp.dtype(x.dtype)
    return math.prod(x.shape) * dtype.itemsize


def call(kernel, pos, ins, outs, scratch=(), spare=4, copies=0, far=""):
    near = pl.BlockSpec(memory_space=pltpu.VMEM)
    hbm = pl.BlockSpec(memory_space=pltpu.HBM)
    if copies:
        scratch = [pltpu.SemaphoreType.DMA((copies,))]
        need = sum(size_of(x) for x in (ins if far == "outs" else outs))
    else:
        need = sum(size_of(x) for x in (*ins, *outs, *scratch))
    if far == "ins":
        ins = [pltpu.with_memory_space_constraint(x, pltpu.HBM) for x in ins]
    return pl.pallas_call(
        kernel,
        in_specs=[pl.BlockSpec(memory_space=pltpu.SMEM)]
        + [hbm if far == "ins" else near] * len(ins),
        out_specs=[hbm if far == "outs" else near] * len(outs),
        out_shape=list(outs),
        scratch_shapes=list(scratch),
        compiler_params=pltpu.CompilerParams(vmem_limit_bytes=need + spare * 2**20),
    )(pos, *ins)


class Plan:
    def __init__(self, devices, tokens_here, head_count, head_size, rank):
        self.inner = math.gcd(head_count // HEADS_PER_DEVICE, devices)
        self.outer = devices // self.inner
        self.heads = head_count // self.inner
        self.tokens = tokens_here
        self.group = tokens_here * self.inner
        self.head_size = head_size
        self.rank = rank
        self.pair = 2 * head_size
        self.width = self.heads * self.pair
        self.rows = rank // self.outer
        self.margin = SEG // 2
        self.scale = head_size ** (-0.5)


def run_copies(sems, moves):
    copies = [pltpu.make_async_copy(a, b, sems.at[i]) for i, (a, b) in enumerate(moves)]
    for copy in copies:
        copy.start()
    for copy in copies:
        copy.wait()


def head_slices(plan, other, h):
    return pl.ds(pl.multiple_of((other * plan.heads + h) * plan.head_size, plan.head_size), plan.head_size)


def pack_kernel(plan, pos, a_ref, b_ref, *refs):
    outs, sems = refs[:-1], refs[-1]
    hd = plan.head_size
    moves = []
    for k, out in enumerate(outs):
        for h in range(plan.heads):
            cols = head_slices(plan, pos[1] ^ k, h)
            moves.append((a_ref.at[:, cols], out.at[:, pl.ds(2 * h * hd, hd)]))
            moves.append((b_ref.at[:, cols], out.at[:, pl.ds((2 * h + 1) * hd, hd)]))
    run_copies(sems, moves)


def unpack_pair_kernel(plan, pos, *refs):
    ins, proj_ref, (a_ref, b_ref, out_ref, sems) = refs[: plan.inner], refs[plan.inner], refs[plan.inner + 1 :]
    hd = plan.head_size
    moves = [(proj_ref, out_ref)]
    for k, src in enumerate(ins):
        for h in range(plan.heads):
            cols = head_slices(plan, pos[1] ^ k, h)
            moves.append((src.at[:, pl.ds(2 * h * hd, hd)], a_ref.at[:, cols]))
            moves.append((src.at[:, pl.ds((2 * h + 1) * hd, hd)], b_ref.at[:, cols]))
    run_copies(sems, moves)


def unpack_kernel(plan, pos, *refs):
    ins, a_ref, sems = refs[: plan.inner], refs[plan.inner], refs[plan.inner + 1]
    wide = plan.heads * plan.head_size
    moves = []
    for k, src in enumerate(ins):
        cols = pl.ds(pl.multiple_of((pos[1] ^ k) * wide, wide), wide)
        moves.append((src, a_ref.at[:, cols]))
    run_copies(sems, moves)


def column_of(mask, row):
    return jnp.sum(jnp.where(mask, row, 0.0), axis=1, keepdims=True)


def head_part(plan, h, pieces, w_ref, logit_ref, expo_ref, floor):
    hd, pair, rank, tokens = plan.head_size, plan.pair, plan.rank, plan.tokens
    top = jnp.broadcast_to(floor, (8, rank))
    for i, src in enumerate(pieces):
        block = dot_nn(src[:, h * pair : h * pair + hd], w_ref[h])
        logit_ref[i * tokens : (i + 1) * tokens, :] = block
        top = jnp.maximum(top, jnp.max(block.reshape(tokens // 8, 8, rank), axis=0))
    top = jnp.max(top, axis=0, keepdims=True)

    def expo_step(i, total):
        at = pl.multiple_of(i * SEG, SEG)
        block = jnp.exp(logit_ref[pl.ds(at, SEG), :] - top)
        expo_ref[pl.ds(at, SEG), :] = block.astype(BF)
        return total + jnp.sum(block.reshape(SEG // 8, 8, rank), axis=0)

    steps = len(pieces) * tokens // SEG
    total = lax.fori_loop(0, steps, expo_step, jnp.zeros((8, rank), FL))
    both = jnp.concatenate([src[:, h * pair : (h + 1) * pair] for src in pieces], axis=0)
    return top, jnp.sum(total, axis=0, keepdims=True), dot_tn(expo_ref[...], both)


def stats_early_kernel(plan, pos, *refs):
    pieces, (w_ref, part_ref, stat_ref, logit_ref, expo_ref) = refs[:-5], refs[-5:]
    heads = plan.heads
    stat_ref[2 * heads :, :] = jnp.zeros((STAT_ROWS - 2 * heads, plan.rank), FL)
    floor = jnp.full((1, plan.rank), -jnp.inf, FL)
    for h in range(heads):
        top, total, part = head_part(plan, h, pieces, w_ref, logit_ref, expo_ref, floor)
        stat_ref[h : h + 1, :] = top
        stat_ref[heads + h : heads + h + 1, :] = total
        part_ref[h] = part


def stats_late_kernel(plan, pos, *refs):
    inner, outer, heads, rank, rows = plan.inner, plan.outer, plan.heads, plan.rank, plan.rows
    pieces, (w_ref, old_ref, old_stat_ref, first_ref, last_ref), refs = (
        refs[:inner],
        refs[inner : inner + 5],
        refs[inner + 5 :],
    )
    outs, (logit_ref, expo_ref, part_ref) = refs[:outer], refs[outer:]
    for k, src in enumerate(pieces):

        @pl.when(pos[1] == k)
        def _():
            first_ref[...] = src[: plan.margin, :]

        @pl.when((pos[1] ^ k) == inner - 1)
        def _():
            last_ref[...] = src[plan.tokens - plan.margin :, :]

    same = lax.broadcasted_iota(jnp.int32, (rank, rank), 0) == lax.broadcasted_iota(
        jnp.int32, (rank, rank), 1
    )
    tops, totals = [], []
    for h in range(heads):
        old_top = old_stat_ref[h : h + 1, :]
        top, total, part = head_part(
            plan, h, pieces[late_from(inner) :], w_ref, logit_ref, expo_ref, old_top
        )
        weight = jnp.exp(old_top - top)
        tops.append(top)
        totals.append(total + weight * old_stat_ref[heads + h : heads + h + 1, :])
        part_ref[h] = part + old_ref[h] * column_of(same, weight)
    stats = jnp.concatenate(
        tops + totals + [jnp.zeros((STAT_ROWS - 2 * heads, rank), FL)], axis=0
    )
    for k, out in enumerate(outs):
        row = pl.multiple_of((pos[0] ^ k) * rows, rows)
        for h in range(heads):
            out[h * rows : (h + 1) * rows, :] = part_ref[h, pl.ds(row, rows), :]
        out[heads * rows :, :] = stats


def late_from(inner):
    return inner // 2 + 1


def own_columns(plan, pos):
    row_at = lax.broadcasted_iota(jnp.int32, (plan.rows, plan.rank), 0)
    col_at = lax.broadcasted_iota(jnp.int32, (plan.rows, plan.rank), 1)
    return col_at == row_at + pos[0] * plan.rows


def combine_kernel(plan, pos, *refs):
    ins, (full_ref, half_ref, stat_ref) = refs[: plan.outer], refs[plan.outer :]
    heads, rows = plan.heads, plan.rows
    own = own_columns(plan, pos)
    stats = [r[heads * rows :, :] for r in ins]
    stat_ref[2 * heads :, :] = jnp.zeros((STAT_ROWS - 2 * heads, plan.rank), FL)
    for h in range(heads):
        tops = [stat[h : h + 1, :] for stat in stats]
        top = tops[0]
        for t in tops[1:]:
            top = jnp.maximum(top, t)
        weights = [jnp.exp(t - top) for t in tops]
        total = weights[0] * stats[0][heads + h : heads + h + 1, :]
        for w, stat in zip(weights[1:], stats[1:]):
            total = total + w * stat[heads + h : heads + h + 1, :]
        inverse = 1.0 / total
        stat_ref[h : h + 1, :] = top
        stat_ref[heads + h : heads + h + 1, :] = inverse
        here = slice(h * rows, (h + 1) * rows)
        result = ins[0][here, :] * column_of(own, weights[0])
        for w, r in zip(weights[1:], ins[1:]):
            result = result + r[here, :] * column_of(own, w)
        result = result * column_of(own, inverse)
        full_ref[here, :] = result
        half_ref[here, :] = result.astype(BF)


def attend_kernel(plan, total_groups, pos, *refs):
    outer, inner, heads = plan.outer, plan.inner, plan.heads
    kv_refs, (before_ref, after_ref), refs = refs[:inner], refs[inner : inner + 2], refs[inner + 2 :]
    bars, qg, refs = refs[:outer], refs[outer : outer + inner], refs[outer + inner :]
    dq_outs, bar_outs, refs = refs[:inner], refs[inner : inner + outer], refs[inner + outer :]
    acc_ref, wg_before_ref, wg_after_ref, ext_ref, bar_ref, q_ref, dbar_ref, dq_ref = refs
    hd, pair, rank, margin, group = plan.head_size, plan.pair, plan.rank, plan.margin, plan.group
    rows = plan.rows
    ext_ref[:margin, :] = before_ref[...]
    for k, src in enumerate(kv_refs):
        row = pl.multiple_of((pos[1] ^ k) * plan.tokens + margin, margin)
        ext_ref[pl.ds(row, plan.tokens), :] = src[...]
    ext_ref[margin + group :, :] = after_ref[...]
    for k, src in enumerate(bars):
        row = pl.multiple_of((pos[0] ^ k) * rows, rows)
        for h in range(heads):
            bar_ref[h, pl.ds(row, rows), :] = src[h * rows : (h + 1) * rows, :]
    for k, src in enumerate(qg):
        row = pl.multiple_of((pos[1] ^ k) * plan.tokens, plan.tokens)
        q_ref[pl.ds(row, plan.tokens), :] = src[...]
    acc_ref[:SEG, :] = jnp.zeros((SEG, plan.width), FL)
    dbar_ref[...] = jnp.zeros(dbar_ref.shape, FL)
    segs = group // SEG
    at_start = pos[0] == 0
    at_end = pos[0] == total_groups - 1
    factor = plan.scale / math.log(2.0)

    def step(j, carry):
        row = pl.multiple_of(j * SEG, SEG)
        hide_low = jnp.where(jnp.logical_and(at_start, j == 0), HIDDEN, 0.0)
        hide_high = jnp.where(jnp.logical_and(at_end, j == segs - 1), HIDDEN, 0.0)
        loaded, scored = [], []
        for h in range(heads):
            low, mid, high = h * pair, h * pair + hd, (h + 1) * pair
            key = jnp.concatenate([bar_ref[h, :, :hd], ext_ref[pl.ds(row, 2 * SEG), low:mid]], axis=0)
            val = jnp.concatenate([bar_ref[h, :, hd:], ext_ref[pl.ds(row, 2 * SEG), mid:high]], axis=0)
            query = q_ref[pl.ds(row, SEG), low:mid]
            grad = q_ref[pl.ds(row, SEG), mid:high]
            loaded.append((key, query, grad))
            scored.append((dot_nt(key, query), dot_nt(val, grad)))
        for h in range(heads):
            low, mid, high = h * pair, h * pair + hd, (h + 1) * pair
            key, query, grad = loaded[h]
            scores, dprob = scored[h]
            scores = jnp.concatenate(
                [
                    scores[:rank],
                    scores[rank : rank + margin] + hide_low,
                    scores[rank + margin : rank + 2 * SEG - margin],
                    scores[rank + 2 * SEG - margin :] + hide_high,
                ],
                axis=0,
            )
            expo = jnp.exp2((scores - jnp.max(scores, axis=0, keepdims=True)) * factor)
            prob = expo * (1.0 / jnp.sum(expo, axis=0, keepdims=True))
            prob_b = prob.astype(BF)
            row_dot = jnp.sum(prob_b.astype(FL) * dprob, axis=0, keepdims=True)
            dscore = (prob * (dprob - row_dot)).astype(BF)
            dquery = dot_tn(key, dscore) * plan.scale
            dq_ref[pl.ds(row, SEG), h * hd : (h + 1) * hd] = jnp.transpose(dquery).astype(BF)
            dkey = dot_nn(dscore, query)
            dval = dot_nn(prob_b, grad)
            dbar_ref[h, :, :hd] += dkey[:rank, :]
            dbar_ref[h, :, hd:] += dval[:rank, :]
            new = pl.multiple_of(row + SEG, SEG)
            acc_ref[pl.ds(row, SEG), low:mid] += dkey[rank : rank + SEG, :]
            acc_ref[pl.ds(row, SEG), mid:high] += dval[rank : rank + SEG, :]
            acc_ref[pl.ds(new, SEG), low:mid] = dkey[rank + SEG :, :]
            acc_ref[pl.ds(new, SEG), mid:high] = dval[rank + SEG :, :]
        return carry

    lax.fori_loop(0, segs, step, 0)
    for h in range(heads):
        low, mid, high = h * pair, h * pair + hd, (h + 1) * pair
        dbar_ref[h, :, :hd] = dbar_ref[h, :, :hd] * plan.scale
        wg_before_ref[:, low:mid] = (acc_ref[:margin, low:mid] * plan.scale).astype(BF)
        wg_before_ref[:, mid:high] = acc_ref[:margin, mid:high].astype(BF)
        wg_after_ref[:, low:mid] = (acc_ref[margin + group :, low:mid] * plan.scale).astype(BF)
        wg_after_ref[:, mid:high] = acc_ref[margin + group :, mid:high].astype(BF)
    for k, out in enumerate(dq_outs):
        row = pl.multiple_of((pos[1] ^ k) * plan.tokens, plan.tokens)
        out[...] = dq_ref[pl.ds(row, plan.tokens), :]
    for k, out in enumerate(bar_outs):
        row = pl.multiple_of((pos[0] ^ k) * rows, rows)
        for h in range(heads):
            out[h * rows : (h + 1) * rows, :] = dbar_ref[h, pl.ds(row, rows), :].astype(BF)


def combine_grad_kernel(plan, pos, *refs):
    full_ref, ins = refs[0], refs[1 : 1 + plan.outer]
    out_ref = refs[1 + plan.outer]
    heads, rows = plan.heads, plan.rows
    total = ins[0][...].astype(FL)
    for r in ins[1:]:
        total = total + r[...].astype(FL)
    half = total.astype(BF)
    out_ref[: heads * rows, :] = half
    column = jnp.sum(full_ref[...] * half.astype(FL), axis=1, keepdims=True)
    own = own_columns(plan, pos)
    parts = []
    for h in range(heads):
        rest = jnp.sum(jnp.where(own, column[h * rows : (h + 1) * rows, :], 0.0), axis=0, keepdims=True)
        for _ in range(3):
            part = rest.astype(BF).astype(FL)
            parts.append(part)
            rest = rest - part
    parts.append(jnp.zeros((DOT_ROWS - 3 * heads, plan.rank), FL))
    out_ref[heads * rows :, :] = jnp.concatenate(parts, axis=0).astype(BF)


def finish_kernel(plan, wave, pos, *refs):
    outer, heads, count = plan.outer, plan.heads, len(wave)
    kv_refs, refs = refs[:count], refs[count:]
    w_ref, stat_ref, wg_ref, before_ref, after_ref = refs[:5]
    bars, refs = refs[5 : 5 + outer], refs[5 + outer :]
    outs, (logit_grad_ref, bar_ref, sum_ref) = refs[:count], refs[count:]
    hd, pair, rank, margin, rows = plan.head_size, plan.pair, plan.rank, plan.margin, plan.rows
    dots = [jnp.zeros((1, rank), FL)] * heads
    for k, src in enumerate(bars):
        row = pl.multiple_of((pos[0] ^ k) * rows, rows)
        sent = src[heads * rows :, :].astype(FL)
        for h in range(heads):
            bar_ref[h, pl.ds(row, rows), :] = src[h * rows : (h + 1) * rows, :]
            dots[h] = dots[h] + jnp.sum(sent[3 * h : 3 * h + 3, :], axis=0, keepdims=True)
    subs = plan.tokens // SEG
    for i, k in enumerate(wave):
        piece_at = pos[1] ^ k
        for sub in range(subs):
            here = slice(sub * SEG, (sub + 1) * SEG)
            from_row = pl.multiple_of(piece_at * plan.tokens + sub * SEG + margin, margin)
            for h in range(heads):
                low, mid, high = h * pair, h * pair + hd, (h + 1) * pair
                both = kv_refs[i][here, low:high]
                dbar = bar_ref[h]
                top = stat_ref[h : h + 1, :]
                inverse = stat_ref[heads + h : heads + h + 1, :]
                expo = jnp.exp(dot_nn(both[:, :hd], w_ref[h]) - top).astype(BF).astype(FL)
                prob = expo * inverse
                dprob = dot_nt(both, dbar)
                logit_grad = (prob * (dprob - dots[h])).astype(BF)
                lines = slice(i * plan.tokens + sub * SEG, i * plan.tokens + (sub + 1) * SEG)
                logit_grad_ref[lines, h * rank : (h + 1) * rank] = logit_grad
                from_prob = dot_nn(prob.astype(BF), dbar)
                window_key = wg_ref[pl.ds(from_row, SEG), low:mid] * plan.scale
                sum_ref[h, :, :hd] = from_prob[:, :hd] + window_key + dot_nt(logit_grad, w_ref[h])
                sum_ref[h, :, hd:] = from_prob[:, hd:] + wg_ref[pl.ds(from_row, SEG), mid:high]
            if sub == 0:

                @pl.when(piece_at == 0)
                def _():
                    for h in range(heads):
                        edge = before_ref[:, h * pair : (h + 1) * pair]
                        sum_ref[h, :margin, :] += edge.astype(FL)

            if sub == subs - 1:

                @pl.when(piece_at == plan.inner - 1)
                def _():
                    for h in range(heads):
                        edge = after_ref[:, h * pair : (h + 1) * pair]
                        sum_ref[h, SEG - margin :, :] += edge.astype(FL)

            for h in range(heads):
                outs[i][here, h * pair : (h + 1) * pair] = sum_ref[h].astype(BF)


def proj_kernel(plan, waves, pos, *refs):
    heads, hd, pair, rank = plan.heads, plan.head_size, plan.pair, plan.rank
    kv_refs, refs = refs[: plan.inner], refs[plan.inner :]
    grad_refs, refs = refs[: len(waves)], refs[len(waves) :]
    outs, proj_ref = refs[: plan.outer], refs[plan.outer]
    for h in range(heads):
        total = jnp.zeros((hd, rank), FL)
        for wave, grad_ref in zip(waves, grad_refs):
            key = jnp.concatenate([kv_refs[k][:, h * pair : h * pair + hd] for k in wave], axis=0)
            total = total + dot_tn(key, grad_ref[:, h * rank : (h + 1) * rank])
        proj_ref[h * hd : (h + 1) * hd, :] = total
    piece = heads * hd // plan.outer
    for k, out in enumerate(outs):
        row = pl.multiple_of((pos[0] ^ k) * piece, piece)
        out[...] = proj_ref[pl.ds(row, piece), :]


def finish_waves(inner):
    quarter = inner // 4
    return (
        tuple(range(inner - quarter, inner)),
        tuple(range(quarter, inner - quarter)),
        tuple(range(quarter)),
    )


def put(items, which, values):
    for k, value in zip(which, values):
        items[k] = value


def exchange(fields, devices, stride, which=None):
    out = []
    for k, field in zip(which or range(len(fields)), fields):
        flip = [(i, i ^ (k * stride)) for i in range(devices)]
        out.append(lax.ppermute(field, "seq", flip) if k else field)
    return out


def swap_edges(upward, downward, devices, stride):
    up = [(i, i + stride) for i in range(devices - stride)]
    down = [(j, i) for i, j in up]
    return lax.ppermute(upward, "seq", up), lax.ppermute(downward, "seq", down)


def per_device(queries, keys, values, grad_out, proj_weight):
    tokens_here, row_width = queries.shape
    head_count, head_size, rank = proj_weight.shape
    devices = lax.axis_size("seq")
    plan = Plan(devices, tokens_here, head_count, head_size, rank)
    inner, outer, heads = plan.inner, plan.outer, plan.heads
    group, width, rows, margin = plan.group, plan.width, plan.rows, plan.margin
    me = lax.axis_index("seq")
    pos = jnp.stack([me // inner, me % inner]).astype(jnp.int32)

    def bind(kernel, *more):
        return lambda pos_ref, *refs: kernel(plan, *more, pos_ref, *refs)

    weight = lax.dynamic_slice_in_dim(proj_weight, (me % inner) * heads, heads, axis=0)
    pair = plan.pair
    piece = struct((tokens_here, width), BF)

    waves = finish_waves(inner)

    def pack(first, second):
        return call(
            bind(pack_kernel),
            pos,
            [first, second],
            [piece] * inner,
            copies=2 * inner * heads,
            far="ins",
        )

    kv_pieces = exchange(pack(keys, values), devices, 1)
    qg_pieces = exchange(pack(queries, grad_out), devices, 1)

    early = late_from(inner)
    old_part, old_stat = call(
        bind(stats_early_kernel),
        pos,
        [*kv_pieces[:early], weight],
        [struct((heads, rank, pair), FL), struct((STAT_ROWS, rank), FL)],
        [pltpu.VMEM((early * tokens_here, rank), FL), pltpu.VMEM((early * tokens_here, rank), BF)],
    )
    late = inner - early
    kv_first, kv_last, *part_send = call(
        bind(stats_late_kernel),
        pos,
        [*kv_pieces, weight, old_part, old_stat],
        [struct((margin, width), BF)] * 2
        + [struct((heads * rows + STAT_ROWS, pair), FL)] * outer,
        [
            pltpu.VMEM((late * tokens_here, rank), FL),
            pltpu.VMEM((late * tokens_here, rank), BF),
            pltpu.VMEM((heads, rank, pair), FL),
        ],
    )
    parts = exchange(part_send, devices, inner)
    kv_before, kv_after = swap_edges(kv_last, kv_first, devices, inner)
    bar_full, bar_half, stats = call(
        bind(combine_kernel),
        pos,
        parts,
        [
            struct((heads * rows, pair), FL),
            struct((heads * rows, pair), BF),
            struct((STAT_ROWS, rank), FL),
        ],
    )
    bars = exchange([bar_half] * outer, devices, inner)

    edge = struct((margin, width), BF)
    results = call(
        bind(attend_kernel, outer),
        pos,
        [*kv_pieces, kv_before, kv_after, *bars, *qg_pieces],
        [struct((tokens_here, heads * head_size), BF)] * inner
        + [struct((heads * rows, pair), BF)] * outer
        + [struct((group + 2 * margin, width), FL), edge, edge],
        [
            pltpu.VMEM((group + 2 * margin, width), BF),
            pltpu.VMEM((heads, rank, pair), BF),
            pltpu.VMEM((group, width), BF),
            pltpu.VMEM((heads, rank, pair), FL),
            pltpu.VMEM((group, heads * head_size), BF),
        ],
    )
    dq_send = results[:inner]
    dbar_send = results[inner : inner + outer]
    wg, wg_before, wg_after = results[inner + outer :]
    dbar_parts = exchange(dbar_send, devices, inner)
    wg_from_before, wg_from_after = swap_edges(wg_after, wg_before, devices, inner)
    (dbar_half,) = call(
        bind(combine_grad_kernel),
        pos,
        [bar_full, *dbar_parts],
        [struct((heads * rows + DOT_ROWS, pair), BF)],
    )
    dbars = exchange([dbar_half] * outer, devices, inner)
    dq_pieces = exchange(dq_send, devices, 1)

    dkv_pieces, logit_grads = [None] * inner, []
    for wave in waves:
        *dkv_send, logit_grad = call(
            bind(finish_kernel, wave),
            pos,
            [*(kv_pieces[k] for k in wave), weight, stats, wg, wg_from_before, wg_from_after, *dbars],
            [piece] * len(wave) + [struct((len(wave) * tokens_here, heads * rank), BF)],
            [pltpu.VMEM((heads, rank, pair), BF), pltpu.VMEM((heads, SEG, pair), FL)],
        )
        logit_grads.append(logit_grad)
        put(dkv_pieces, wave, exchange(dkv_send, devices, 1, wave))
    proj_send = call(
        bind(proj_kernel, waves),
        pos,
        [*kv_pieces, *logit_grads],
        [struct((heads * head_size // outer, rank), FL)] * outer,
        [pltpu.VMEM((heads * head_size, rank), FL)],
    )
    proj_parts = exchange(proj_send, devices, inner)
    proj_sum = proj_parts[0]
    for part in proj_parts[1:]:
        proj_sum = proj_sum + part
    place = [(o * inner + p, p * outer + o) for o in range(outer) for p in range(inner)]
    proj_here = lax.ppermute(proj_sum, "seq", place)
    whole = struct((tokens_here, row_width), BF)
    (grad_queries,) = call(bind(unpack_kernel), pos, dq_pieces, [whole], copies=inner, far="outs")
    grad_keys, grad_values, grad_proj = call(
        bind(unpack_pair_kernel),
        pos,
        [*dkv_pieces, proj_here],
        [whole, whole, struct(proj_here.shape, FL)],
        copies=2 * inner * heads + 1,
        far="outs",
    )
    return (grad_queries, grad_keys, grad_values, grad_proj)


def solution(mesh):
    in_specs = (P("seq", None), P("seq", None), P("seq", None), P("seq", None), P())
    out_specs = (P("seq", None), P("seq", None), P("seq", None), P("seq", None))
    return jax.shard_map(
        per_device, mesh=mesh, in_specs=in_specs, out_specs=out_specs, check_vma=False
    )
```

```python
import math

import jax
import jax.numpy as jnp
from jax import lax
from jax.experimental import pallas as pl
from jax.experimental.pallas import tpu as pltpu
from jax.sharding import PartitionSpec as P


SEG = 256
STAT_ROWS = 8
DOT_ROWS = 16
HIDDEN = -1e30
HEADS_PER_DEVICE = 2
BF = jnp.bfloat16
FL = jnp.float32


def dot_nn(a, b):
    return lax.dot_general(a, b, (((1,), (0,)), ((), ())), preferred_element_type=FL)


def dot_nt(a, b):
    return lax.dot_general(a, b, (((1,), (1,)), ((), ())), preferred_element_type=FL)


def dot_tn(a, b):
    return lax.dot_general(a, b, (((0,), (0,)), ((), ())), preferred_element_type=FL)


def struct(shape, dtype):
    return jax.ShapeDtypeStruct(shape, dtype)


def size_of(x):
    dtype = jnp.dtype(x.dtype)
    return math.prod(x.shape) * dtype.itemsize


def call(kernel, pos, ins, outs, scratch=(), spare=4, far=""):
    near = pl.BlockSpec(memory_space=pltpu.VMEM)
    hbm = pl.BlockSpec(memory_space=pltpu.HBM)
    held = [x for x in scratch if hasattr(x.dtype, "itemsize")]
    if "ins" in far:
        ins = [pltpu.with_memory_space_constraint(x, pltpu.HBM) for x in ins]
    else:
        held += ins
    if "outs" not in far:
        held += outs
    return pl.pallas_call(
        kernel,
        in_specs=[pl.BlockSpec(memory_space=pltpu.SMEM)] + [hbm if "ins" in far else near] * len(ins),
        out_specs=[hbm if "outs" in far else near] * len(outs),
        out_shape=list(outs),
        scratch_shapes=list(scratch),
        compiler_params=pltpu.CompilerParams(
            vmem_limit_bytes=sum(map(size_of, held)) + spare * 2**20
        ),
    )(pos, *ins)


class Plan:
    def __init__(self, devices, tokens_here, head_count, head_size, rank):
        self.inner = math.gcd(head_count // HEADS_PER_DEVICE, devices)
        self.outer = devices // self.inner
        self.heads = head_count // self.inner
        self.devices = devices
        self.tokens = tokens_here
        self.group = tokens_here * self.inner
        self.head_size = head_size
        self.rank = rank
        self.pair = 2 * head_size
        self.width = self.heads * self.pair
        self.rows = rank // self.outer
        self.margin = SEG // 2
        self.scale = head_size ** (-0.5)


def run_copies(sems, moves):
    copies = [pltpu.make_async_copy(a, b, sems.at[i]) for i, (a, b) in enumerate(moves)]
    for copy in copies:
        copy.start()
    for copy in copies:
        copy.wait()


def head_slices(plan, other, h):
    return pl.ds(pl.multiple_of((other * plan.heads + h) * plan.head_size, plan.head_size), plan.head_size)


def pack_kernel(plan, pos, a_ref, b_ref, *refs):
    outs, (in_sems, out_sems, buffer) = refs[: plan.inner], refs[plan.inner :]
    hd = plan.head_size
    coming, leaving = [], []
    for k, out in enumerate(outs):
        for h in range(plan.heads):
            cols = head_slices(plan, pos[1] ^ k, h)
            for side, src in enumerate((a_ref, b_ref)):
                at = 2 * h + side
                coming.append(
                    pltpu.make_async_copy(
                        src.at[:, cols],
                        buffer.at[k, :, pl.ds(at * hd, hd)],
                        in_sems.at[2 * plan.heads * k + at],
                    )
                )
        leaving.append(pltpu.make_async_copy(buffer.at[k], out, out_sems.at[k]))
    for copy in coming:
        copy.start()
    for k in range(plan.inner):
        for copy in coming[2 * plan.heads * k : 2 * plan.heads * (k + 1)]:
            copy.wait()
        leaving[k].start()
    for copy in leaving:
        copy.wait()


def unpack_pair_kernel(plan, pos, *refs):
    ins, proj_ref, (a_ref, b_ref, out_ref, sems) = refs[: plan.inner], refs[plan.inner], refs[plan.inner + 1 :]
    hd = plan.head_size
    moves = [(proj_ref, out_ref)]
    for k, src in enumerate(ins):
        for h in range(plan.heads):
            cols = head_slices(plan, pos[1] ^ k, h)
            moves.append((src.at[:, pl.ds(2 * h * hd, hd)], a_ref.at[:, cols]))
            moves.append((src.at[:, pl.ds((2 * h + 1) * hd, hd)], b_ref.at[:, cols]))
    run_copies(sems, moves)


def unpack_kernel(plan, pos, *refs):
    ins, a_ref, sems = refs[: plan.inner], refs[plan.inner], refs[plan.inner + 1]
    wide = plan.heads * plan.head_size
    moves = []
    for k, src in enumerate(ins):
        cols = pl.ds(pl.multiple_of((pos[1] ^ k) * wide, wide), wide)
        moves.append((src, a_ref.at[:, cols]))
    run_copies(sems, moves)


def column_of(mask, row):
    return jnp.sum(jnp.where(mask, row, 0.0), axis=1, keepdims=True)


def head_part(plan, h, pieces, w_ref, logit_ref, expo_ref, floor):
    hd, pair, rank, tokens = plan.head_size, plan.pair, plan.rank, plan.tokens
    top = jnp.broadcast_to(floor, (8, rank))
    for i, src in enumerate(pieces):
        block = dot_nn(src[:, h * pair : h * pair + hd], w_ref[h])
        logit_ref[i * tokens : (i + 1) * tokens, :] = block
        top = jnp.maximum(top, jnp.max(block.reshape(tokens // 8, 8, rank), axis=0))
    top = jnp.max(top, axis=0, keepdims=True)

    def expo_step(i, total):
        at = pl.multiple_of(i * SEG, SEG)
        block = jnp.exp(logit_ref[pl.ds(at, SEG), :] - top)
        expo_ref[pl.ds(at, SEG), :] = block.astype(BF)
        return total + jnp.sum(block.reshape(SEG // 8, 8, rank), axis=0)

    steps = len(pieces) * tokens // SEG
    total = lax.fori_loop(0, steps, expo_step, jnp.zeros((8, rank), FL))
    both = jnp.concatenate([src[:, h * pair : (h + 1) * pair] for src in pieces], axis=0)
    return top, jnp.sum(total, axis=0, keepdims=True), dot_tn(expo_ref[...], both)


def stats_early_kernel(plan, pos, *refs):
    pieces, (w_ref, part_ref, stat_ref, logit_ref, expo_ref) = refs[:-5], refs[-5:]
    heads = plan.heads
    stat_ref[2 * heads :, :] = jnp.zeros((STAT_ROWS - 2 * heads, plan.rank), FL)
    floor = jnp.full((1, plan.rank), -jnp.inf, FL)
    for h in range(heads):
        top, total, part = head_part(plan, h, pieces, w_ref, logit_ref, expo_ref, floor)
        stat_ref[h : h + 1, :] = top
        stat_ref[heads + h : heads + h + 1, :] = total
        part_ref[h] = part


def stats_late_kernel(plan, pos, *refs):
    inner, outer, heads, rank, rows = plan.inner, plan.outer, plan.heads, plan.rank, plan.rows
    pieces, (w_ref, old_ref, old_stat_ref, first_ref, last_ref), refs = (
        refs[:inner],
        refs[inner : inner + 5],
        refs[inner + 5 :],
    )
    outs, (logit_ref, expo_ref, part_ref) = refs[:outer], refs[outer:]
    for k, src in enumerate(pieces):

        @pl.when(pos[1] == k)
        def _():
            first_ref[...] = src[: plan.margin, :]

        @pl.when((pos[1] ^ k) == inner - 1)
        def _():
            last_ref[...] = src[plan.tokens - plan.margin :, :]

    same = lax.broadcasted_iota(jnp.int32, (rank, rank), 0) == lax.broadcasted_iota(
        jnp.int32, (rank, rank), 1
    )
    tops, totals = [], []
    for h in range(heads):
        old_top = old_stat_ref[h : h + 1, :]
        top, total, part = head_part(
            plan, h, pieces[late_from(inner) :], w_ref, logit_ref, expo_ref, old_top
        )
        weight = jnp.exp(old_top - top)
        tops.append(top)
        totals.append(total + weight * old_stat_ref[heads + h : heads + h + 1, :])
        part_ref[h] = part + old_ref[h] * column_of(same, weight)
    stats = jnp.concatenate(
        tops + totals + [jnp.zeros((STAT_ROWS - 2 * heads, rank), FL)], axis=0
    )
    for k, out in enumerate(outs):
        row = pl.multiple_of((pos[0] ^ k) * rows, rows)
        for h in range(heads):
            out[h * rows : (h + 1) * rows, :] = part_ref[h, pl.ds(row, rows), :]
        out[heads * rows :, :] = stats


def late_from(inner):
    return inner // 2 + 1


def own_columns(plan, pos):
    row_at = lax.broadcasted_iota(jnp.int32, (plan.rows, plan.rank), 0)
    col_at = lax.broadcasted_iota(jnp.int32, (plan.rows, plan.rank), 1)
    return col_at == row_at + pos[0] * plan.rows


def combine_kernel(plan, pos, *refs):
    ins, (full_ref, half_ref, stat_ref) = refs[: plan.outer], refs[plan.outer :]
    heads, rows = plan.heads, plan.rows
    own = own_columns(plan, pos)
    stats = [r[heads * rows :, :] for r in ins]
    stat_ref[2 * heads :, :] = jnp.zeros((STAT_ROWS - 2 * heads, plan.rank), FL)
    for h in range(heads):
        tops = [stat[h : h + 1, :] for stat in stats]
        top = tops[0]
        for t in tops[1:]:
            top = jnp.maximum(top, t)
        weights = [jnp.exp(t - top) for t in tops]
        total = weights[0] * stats[0][heads + h : heads + h + 1, :]
        for w, stat in zip(weights[1:], stats[1:]):
            total = total + w * stat[heads + h : heads + h + 1, :]
        inverse = 1.0 / total
        stat_ref[h : h + 1, :] = top
        stat_ref[heads + h : heads + h + 1, :] = inverse
        here = slice(h * rows, (h + 1) * rows)
        result = ins[0][here, :] * column_of(own, weights[0])
        for w, r in zip(weights[1:], ins[1:]):
            result = result + r[here, :] * column_of(own, w)
        result = result * column_of(own, inverse)
        full_ref[here, :] = result
        half_ref[here, :] = result.astype(BF)


def attend_kernel(plan, total_groups, pos, *refs):
    outer, inner, heads = plan.outer, plan.inner, plan.heads
    kv_refs, (before_ref, after_ref), refs = refs[:inner], refs[inner : inner + 2], refs[inner + 2 :]
    bars, qg, refs = refs[:outer], refs[outer : outer + inner], refs[outer + inner :]
    dq_outs, bar_outs, refs = refs[:inner], refs[inner : inner + outer], refs[inner + outer :]
    acc_ref, wg_before_ref, wg_after_ref, ext_ref, bar_ref, q_ref, dbar_ref, dq_ref = refs
    hd, pair, rank, margin, group = plan.head_size, plan.pair, plan.rank, plan.margin, plan.group
    rows = plan.rows
    ext_ref[:margin, :] = before_ref[...]
    for k, src in enumerate(kv_refs):
        row = pl.multiple_of((pos[1] ^ k) * plan.tokens + margin, margin)
        ext_ref[pl.ds(row, plan.tokens), :] = src[...]
    ext_ref[margin + group :, :] = after_ref[...]
    for k, src in enumerate(bars):
        row = pl.multiple_of((pos[0] ^ k) * rows, rows)
        for h in range(heads):
            bar_ref[h, pl.ds(row, rows), :] = src[h * rows : (h + 1) * rows, :]
    for k, src in enumerate(qg):
        row = pl.multiple_of((pos[1] ^ k) * plan.tokens, plan.tokens)
        q_ref[pl.ds(row, plan.tokens), :] = src[...]
    acc_ref[:SEG, :] = jnp.zeros((SEG, plan.width), FL)
    dbar_ref[...] = jnp.zeros(dbar_ref.shape, FL)
    segs = group // SEG
    at_start = pos[0] == 0
    at_end = pos[0] == total_groups - 1
    factor = plan.scale / math.log(2.0)

    def step(j, carry):
        row = pl.multiple_of(j * SEG, SEG)
        hide_low = jnp.where(jnp.logical_and(at_start, j == 0), HIDDEN, 0.0)
        hide_high = jnp.where(jnp.logical_and(at_end, j == segs - 1), HIDDEN, 0.0)
        loaded, scored = [], []
        for h in range(heads):
            low, mid, high = h * pair, h * pair + hd, (h + 1) * pair
            key = jnp.concatenate([bar_ref[h, :, :hd], ext_ref[pl.ds(row, 2 * SEG), low:mid]], axis=0)
            val = jnp.concatenate([bar_ref[h, :, hd:], ext_ref[pl.ds(row, 2 * SEG), mid:high]], axis=0)
            query = q_ref[pl.ds(row, SEG), low:mid]
            grad = q_ref[pl.ds(row, SEG), mid:high]
            loaded.append((key, query, grad))
            scored.append((dot_nt(key, query), dot_nt(val, grad)))
        for h in range(heads):
            low, mid, high = h * pair, h * pair + hd, (h + 1) * pair
            key, query, grad = loaded[h]
            scores, dprob = scored[h]
            scores = jnp.concatenate(
                [
                    scores[:rank],
                    scores[rank : rank + margin] + hide_low,
                    scores[rank + margin : rank + 2 * SEG - margin],
                    scores[rank + 2 * SEG - margin :] + hide_high,
                ],
                axis=0,
            )
            expo = jnp.exp2((scores - jnp.max(scores, axis=0, keepdims=True)) * factor)
            prob = expo * (1.0 / jnp.sum(expo, axis=0, keepdims=True))
            prob_b = prob.astype(BF)
            row_dot = jnp.sum(prob_b.astype(FL) * dprob, axis=0, keepdims=True)
            dscore = (prob * (dprob - row_dot)).astype(BF)
            dquery = dot_tn(key, dscore) * plan.scale
            dq_ref[pl.ds(row, SEG), h * hd : (h + 1) * hd] = jnp.transpose(dquery).astype(BF)
            dkey = dot_nn(dscore, query)
            dval = dot_nn(prob_b, grad)
            dbar_ref[h, :, :hd] += dkey[:rank, :]
            dbar_ref[h, :, hd:] += dval[:rank, :]
            new = pl.multiple_of(row + SEG, SEG)
            acc_ref[pl.ds(row, SEG), low:mid] += dkey[rank : rank + SEG, :]
            acc_ref[pl.ds(row, SEG), mid:high] += dval[rank : rank + SEG, :]
            acc_ref[pl.ds(new, SEG), low:mid] = dkey[rank + SEG :, :]
            acc_ref[pl.ds(new, SEG), mid:high] = dval[rank + SEG :, :]
        return carry

    lax.fori_loop(0, segs, step, 0)
    for h in range(heads):
        low, mid, high = h * pair, h * pair + hd, (h + 1) * pair
        dbar_ref[h, :, :hd] = dbar_ref[h, :, :hd] * plan.scale
        wg_before_ref[:, low:mid] = (acc_ref[:margin, low:mid] * plan.scale).astype(BF)
        wg_before_ref[:, mid:high] = acc_ref[:margin, mid:high].astype(BF)
        wg_after_ref[:, low:mid] = (acc_ref[margin + group :, low:mid] * plan.scale).astype(BF)
        wg_after_ref[:, mid:high] = acc_ref[margin + group :, mid:high].astype(BF)
    for k, out in enumerate(dq_outs):
        row = pl.multiple_of((pos[1] ^ k) * plan.tokens, plan.tokens)
        out[...] = dq_ref[pl.ds(row, plan.tokens), :]
    for k, out in enumerate(bar_outs):
        row = pl.multiple_of((pos[0] ^ k) * rows, rows)
        for h in range(heads):
            out[h * rows : (h + 1) * rows, :] = dbar_ref[h, pl.ds(row, rows), :].astype(BF)


def combine_grad_kernel(plan, pos, *refs):
    full_ref, ins = refs[0], refs[1 : 1 + plan.outer]
    out_ref = refs[1 + plan.outer]
    heads, rows = plan.heads, plan.rows
    total = ins[0][...].astype(FL)
    for r in ins[1:]:
        total = total + r[...].astype(FL)
    half = total.astype(BF)
    out_ref[: heads * rows, :] = half
    column = jnp.sum(full_ref[...] * half.astype(FL), axis=1, keepdims=True)
    own = own_columns(plan, pos)
    parts = []
    for h in range(heads):
        rest = jnp.sum(jnp.where(own, column[h * rows : (h + 1) * rows, :], 0.0), axis=0, keepdims=True)
        for _ in range(3):
            part = rest.astype(BF).astype(FL)
            parts.append(part)
            rest = rest - part
    parts.append(jnp.zeros((DOT_ROWS - 3 * heads, plan.rank), FL))
    out_ref[heads * rows :, :] = jnp.concatenate(parts, axis=0).astype(BF)


def finish_kernel(plan, wave, pos, *refs):
    outer, heads, count = plan.outer, plan.heads, len(wave)
    kv_refs, refs = refs[:count], refs[count:]
    w_ref, stat_ref, wg_ref, before_ref, after_ref = refs[:5]
    bars, refs = refs[5 : 5 + outer], refs[5 + outer :]
    outs, (logit_grad_ref, bar_ref, sum_ref) = refs[:count], refs[count:]
    hd, pair, rank, margin, rows = plan.head_size, plan.pair, plan.rank, plan.margin, plan.rows
    dots = [jnp.zeros((1, rank), FL)] * heads
    for k, src in enumerate(bars):
        row = pl.multiple_of((pos[0] ^ k) * rows, rows)
        sent = src[heads * rows :, :].astype(FL)
        for h in range(heads):
            bar_ref[h, pl.ds(row, rows), :] = src[h * rows : (h + 1) * rows, :]
            dots[h] = dots[h] + jnp.sum(sent[3 * h : 3 * h + 3, :], axis=0, keepdims=True)
    subs = plan.tokens // SEG
    for i, k in enumerate(wave):
        piece_at = pos[1] ^ k
        for sub in range(subs):
            here = slice(sub * SEG, (sub + 1) * SEG)
            from_row = pl.multiple_of(piece_at * plan.tokens + sub * SEG + margin, margin)
            for h in range(heads):
                low, mid, high = h * pair, h * pair + hd, (h + 1) * pair
                both = kv_refs[i][here, low:high]
                dbar = bar_ref[h]
                top = stat_ref[h : h + 1, :]
                inverse = stat_ref[heads + h : heads + h + 1, :]
                expo = jnp.exp(dot_nn(both[:, :hd], w_ref[h]) - top).astype(BF).astype(FL)
                prob = expo * inverse
                dprob = dot_nt(both, dbar)
                logit_grad = (prob * (dprob - dots[h])).astype(BF)
                lines = slice(i * plan.tokens + sub * SEG, i * plan.tokens + (sub + 1) * SEG)
                logit_grad_ref[lines, h * rank : (h + 1) * rank] = logit_grad
                from_prob = dot_nn(prob.astype(BF), dbar)
                window_key = wg_ref[pl.ds(from_row, SEG), low:mid] * plan.scale
                sum_ref[h, :, :hd] = from_prob[:, :hd] + window_key + dot_nt(logit_grad, w_ref[h])
                sum_ref[h, :, hd:] = from_prob[:, hd:] + wg_ref[pl.ds(from_row, SEG), mid:high]
            if sub == 0:

                @pl.when(piece_at == 0)
                def _():
                    for h in range(heads):
                        edge = before_ref[:, h * pair : (h + 1) * pair]
                        sum_ref[h, :margin, :] += edge.astype(FL)

            if sub == subs - 1:

                @pl.when(piece_at == plan.inner - 1)
                def _():
                    for h in range(heads):
                        edge = after_ref[:, h * pair : (h + 1) * pair]
                        sum_ref[h, SEG - margin :, :] += edge.astype(FL)

            for h in range(heads):
                outs[i][here, h * pair : (h + 1) * pair] = sum_ref[h].astype(BF)


def proj_kernel(plan, waves, pos, *refs):
    heads, hd, pair, rank = plan.heads, plan.head_size, plan.pair, plan.rank
    kv_refs, refs = refs[: plan.inner], refs[plan.inner :]
    grad_refs, refs = refs[: len(waves)], refs[len(waves) :]
    outs, proj_ref = refs[: plan.outer], refs[plan.outer]
    for h in range(heads):
        total = jnp.zeros((hd, rank), FL)
        for wave, grad_ref in zip(waves, grad_refs):
            key = jnp.concatenate([kv_refs[k][:, h * pair : h * pair + hd] for k in wave], axis=0)
            total = total + dot_tn(key, grad_ref[:, h * rank : (h + 1) * rank])
        proj_ref[h * hd : (h + 1) * hd, :] = total
    piece = heads * hd // plan.outer
    for k, out in enumerate(outs):
        row = pl.multiple_of((pos[0] ^ k) * piece, piece)
        out[...] = proj_ref[pl.ds(row, piece), :]


def finish_waves(inner):
    quarter = inner // 4
    return (
        tuple(range(inner - quarter, inner)),
        tuple(range(quarter, inner - quarter)),
        tuple(range(quarter)),
    )


def put(items, which, values):
    for k, value in zip(which, values):
        items[k] = value


def exchange(fields, devices, stride, which=None):
    out = []
    for k, field in zip(which or range(len(fields)), fields):
        flip = [(i, i ^ (k * stride)) for i in range(devices)]
        out.append(lax.ppermute(field, "seq", flip) if k else field)
    return out


def swap_edges(upward, downward, devices, stride):
    up = [(i, i + stride) for i in range(devices - stride)]
    down = [(j, i) for i, j in up]
    return lax.ppermute(upward, "seq", up), lax.ppermute(downward, "seq", down)


def per_device(queries, keys, values, grad_out, proj_weight):
    tokens_here, row_width = queries.shape
    head_count, head_size, rank = proj_weight.shape
    devices = lax.axis_size("seq")
    plan = Plan(devices, tokens_here, head_count, head_size, rank)
    inner, outer, heads = plan.inner, plan.outer, plan.heads
    group, width, rows, margin = plan.group, plan.width, plan.rows, plan.margin
    me = lax.axis_index("seq")
    pos = jnp.stack([me // inner, me % inner]).astype(jnp.int32)

    def bind(kernel, *more):
        return lambda pos_ref, *refs: kernel(plan, *more, pos_ref, *refs)

    weight = lax.dynamic_slice_in_dim(proj_weight, (me % inner) * heads, heads, axis=0)
    pair = plan.pair
    piece = struct((tokens_here, width), BF)

    waves = finish_waves(inner)

    def pack(first, second):
        return call(
            bind(pack_kernel),
            pos,
            [first, second],
            [piece] * inner,
            [
                pltpu.SemaphoreType.DMA((2 * inner * heads,)),
                pltpu.SemaphoreType.DMA((inner,)),
                pltpu.VMEM((inner, tokens_here, width), BF),
            ],
            far="ins outs",
        )

    kv_pieces = exchange(pack(keys, values), devices, 1)
    qg_pieces = exchange(pack(queries, grad_out), devices, 1)

    early = late_from(inner)
    old_part, old_stat = call(
        bind(stats_early_kernel),
        pos,
        [*kv_pieces[:early], weight],
        [struct((heads, rank, pair), FL), struct((STAT_ROWS, rank), FL)],
        [pltpu.VMEM((early * tokens_here, rank), FL), pltpu.VMEM((early * tokens_here, rank), BF)],
    )
    late = inner - early
    kv_first, kv_last, *part_send = call(
        bind(stats_late_kernel),
        pos,
        [*kv_pieces, weight, old_part, old_stat],
        [struct((margin, width), BF)] * 2
        + [struct((heads * rows + STAT_ROWS, pair), FL)] * outer,
        [
            pltpu.VMEM((late * tokens_here, rank), FL),
            pltpu.VMEM((late * tokens_here, rank), BF),
            pltpu.VMEM((heads, rank, pair), FL),
        ],
    )
    parts = exchange(part_send, devices, inner)
    kv_before, kv_after = swap_edges(kv_last, kv_first, devices, inner)
    bar_full, bar_half, stats = call(
        bind(combine_kernel),
        pos,
        parts,
        [
            struct((heads * rows, pair), FL),
            struct((heads * rows, pair), BF),
            struct((STAT_ROWS, rank), FL),
        ],
    )
    bars = exchange([bar_half] * outer, devices, inner)

    edge = struct((margin, width), BF)
    results = call(
        bind(attend_kernel, outer),
        pos,
        [*kv_pieces, kv_before, kv_after, *bars, *qg_pieces],
        [struct((tokens_here, heads * head_size), BF)] * inner
        + [struct((heads * rows, pair), BF)] * outer
        + [struct((group + 2 * margin, width), FL), edge, edge],
        [
            pltpu.VMEM((group + 2 * margin, width), BF),
            pltpu.VMEM((heads, rank, pair), BF),
            pltpu.VMEM((group, width), BF),
            pltpu.VMEM((heads, rank, pair), FL),
            pltpu.VMEM((group, heads * head_size), BF),
        ],
    )
    dq_send = results[:inner]
    dbar_send = results[inner : inner + outer]
    wg, wg_before, wg_after = results[inner + outer :]
    dbar_parts = exchange(dbar_send, devices, inner)
    wg_from_before, wg_from_after = swap_edges(wg_after, wg_before, devices, inner)
    (dbar_half,) = call(
        bind(combine_grad_kernel), pos, [bar_full, *dbar_parts], [struct((heads * rows + DOT_ROWS, pair), BF)]
    )
    dbars = exchange([dbar_half] * outer, devices, inner)
    dq_pieces = [None] * inner
    first, others = waves[0], tuple(k for k in range(inner) if k not in waves[0])
    put(dq_pieces, first, exchange([dq_send[k] for k in first], devices, 1, first))
    put(dq_pieces, others, exchange([dq_send[k] for k in others], devices, 1, others))

    dkv_pieces, logit_grads = [None] * inner, []
    for wave in waves:
        *dkv_send, logit_grad = call(
            bind(finish_kernel, wave),
            pos,
            [*(kv_pieces[k] for k in wave), weight, stats, wg, wg_from_before, wg_from_after, *dbars],
            [piece] * len(wave) + [struct((len(wave) * tokens_here, heads * rank), BF)],
            [pltpu.VMEM((heads, rank, pair), BF), pltpu.VMEM((heads, SEG, pair), FL)],
        )
        logit_grads.append(logit_grad)
        put(dkv_pieces, wave, exchange(dkv_send, devices, 1, wave))
    proj_send = call(
        bind(proj_kernel, waves),
        pos,
        [*kv_pieces, *logit_grads],
        [struct((heads * head_size // outer, rank), FL)] * outer,
        [pltpu.VMEM((heads * head_size, rank), FL)],
    )
    proj_parts = exchange(proj_send, devices, inner)
    proj_sum = proj_parts[0]
    for part in proj_parts[1:]:
        proj_sum = proj_sum + part
    place = [(o * inner + p, p * outer + o) for o in range(outer) for p in range(inner)]
    proj_here = lax.ppermute(proj_sum, "seq", place)
    whole = struct((tokens_here, row_width), BF)
    (grad_queries,) = call(
        bind(unpack_kernel), pos, dq_pieces, [whole], [pltpu.SemaphoreType.DMA((inner,))], far="outs"
    )
    grad_keys, grad_values, grad_proj = call(
        bind(unpack_pair_kernel),
        pos,
        [*dkv_pieces, proj_here],
        [whole, whole, struct(proj_here.shape, FL)],
        [pltpu.SemaphoreType.DMA((2 * inner * heads + 1,))],
        far="outs",
    )
    return (grad_queries, grad_keys, grad_values, grad_proj)


def solution(mesh):
    in_specs = (P("seq", None), P("seq", None), P("seq", None), P("seq", None), P())
    out_specs = (P("seq", None), P("seq", None), P("seq", None), P("seq", None))
    return jax.shard_map(per_device, mesh=mesh, in_specs=in_specs, out_specs=out_specs, check_vma=False)
```

```python
import math

import jax
import jax.numpy as jnp
from jax import lax
from jax.experimental import pallas as pl
from jax.experimental.pallas import tpu as pltpu
from jax.sharding import PartitionSpec as P


SEG = 256
STAT_ROWS = 8
DOT_ROWS = 16
HIDDEN = -1e30
HEADS_PER_DEVICE = 2
BF = jnp.bfloat16
FL = jnp.float32


def dot_nn(a, b):
    return lax.dot_general(a, b, (((1,), (0,)), ((), ())), preferred_element_type=FL)


def dot_nt(a, b):
    return lax.dot_general(a, b, (((1,), (1,)), ((), ())), preferred_element_type=FL)


def dot_tn(a, b):
    return lax.dot_general(a, b, (((0,), (0,)), ((), ())), preferred_element_type=FL)


def struct(shape, dtype):
    return jax.ShapeDtypeStruct(shape, dtype)


def size_of(x):
    dtype = jnp.dtype(x.dtype)
    return math.prod(x.shape) * dtype.itemsize


def call(kernel, pos, ins, outs, scratch=(), spare=4, far="", aliases=()):
    near = pl.BlockSpec(memory_space=pltpu.VMEM)
    hbm = pl.BlockSpec(memory_space=pltpu.HBM)
    held = [x for x in scratch if hasattr(x.dtype, "itemsize")]
    if "ins" in far:
        ins = [pltpu.with_memory_space_constraint(x, pltpu.HBM) for x in ins]
    else:
        held += [x for i, x in enumerate(ins) if i not in dict(aliases)]
    if "outs" not in far:
        held += outs
    return pl.pallas_call(
        kernel,
        in_specs=[pl.BlockSpec(memory_space=pltpu.SMEM)]
        + [hbm if "ins" in far or i in dict(aliases) else near for i in range(len(ins))],
        out_specs=[hbm if "outs" in far else near] * len(outs),
        out_shape=list(outs),
        scratch_shapes=list(scratch),
        input_output_aliases={i + 1: o for i, o in aliases},
        compiler_params=pltpu.CompilerParams(
            vmem_limit_bytes=sum(map(size_of, held)) + spare * 2**20
        ),
    )(pos, *ins)


class Plan:
    def __init__(self, devices, tokens_here, head_count, head_size, rank):
        self.inner = math.gcd(head_count // HEADS_PER_DEVICE, devices)
        self.outer = devices // self.inner
        self.heads = head_count // self.inner
        self.devices = devices
        self.tokens = tokens_here
        self.group = tokens_here * self.inner
        self.head_size = head_size
        self.rank = rank
        self.pair = 2 * head_size
        self.width = self.heads * self.pair
        self.rows = rank // self.outer
        self.margin = SEG // 2
        self.scale = head_size ** (-0.5)


def run_copies(sems, moves):
    copies = [pltpu.make_async_copy(a, b, sems.at[i]) for i, (a, b) in enumerate(moves)]
    for copy in copies:
        copy.start()
    for copy in copies:
        copy.wait()


def head_slices(plan, other, h):
    return pl.ds(pl.multiple_of((other * plan.heads + h) * plan.head_size, plan.head_size), plan.head_size)


def pack_kernel(plan, pos, a_ref, b_ref, *refs):
    outs, (in_sems, out_sems, buffer) = refs[: plan.inner], refs[plan.inner :]
    hd = plan.head_size
    coming, leaving = [], []
    for k, out in enumerate(outs):
        for h in range(plan.heads):
            cols = head_slices(plan, pos[1] ^ k, h)
            for side, src in enumerate((a_ref, b_ref)):
                at = 2 * h + side
                coming.append(
                    pltpu.make_async_copy(
                        src.at[:, cols],
                        buffer.at[k, :, pl.ds(at * hd, hd)],
                        in_sems.at[2 * plan.heads * k + at],
                    )
                )
        leaving.append(pltpu.make_async_copy(buffer.at[k], out, out_sems.at[k]))
    for copy in coming:
        copy.start()
    for k in range(plan.inner):
        for copy in coming[2 * plan.heads * k : 2 * plan.heads * (k + 1)]:
            copy.wait()
        leaving[k].start()
    for copy in leaving:
        copy.wait()


def unpack_pair_kernel(plan, which, last, pos, *refs):
    ins, refs = refs[: len(which)], refs[len(which) :]
    moves = []
    if last:
        proj_ref, _, _, a_ref, b_ref, out_ref, sems = refs
        moves.append((proj_ref, out_ref))
    else:
        a_ref, b_ref, sems = refs
    hd = plan.head_size
    for k, src in zip(which, ins):
        for h in range(plan.heads):
            cols = head_slices(plan, pos[1] ^ k, h)
            moves.append((src.at[:, pl.ds(2 * h * hd, hd)], a_ref.at[:, cols]))
            moves.append((src.at[:, pl.ds((2 * h + 1) * hd, hd)], b_ref.at[:, cols]))
    run_copies(sems, moves)


def unpack_kernel(plan, pos, *refs):
    ins, a_ref, sems = refs[: plan.inner], refs[plan.inner], refs[plan.inner + 1]
    wide = plan.heads * plan.head_size
    moves = []
    for k, src in enumerate(ins):
        cols = pl.ds(pl.multiple_of((pos[1] ^ k) * wide, wide), wide)
        moves.append((src, a_ref.at[:, cols]))
    run_copies(sems, moves)


def column_of(mask, row):
    return jnp.sum(jnp.where(mask, row, 0.0), axis=1, keepdims=True)


def head_part(plan, h, pieces, w_ref, logit_ref, expo_ref, floor):
    hd, pair, rank, tokens = plan.head_size, plan.pair, plan.rank, plan.tokens
    top = jnp.broadcast_to(floor, (8, rank))
    for i, src in enumerate(pieces):
        block = dot_nn(src[:, h * pair : h * pair + hd], w_ref[h])
        logit_ref[i * tokens : (i + 1) * tokens, :] = block
        top = jnp.maximum(top, jnp.max(block.reshape(tokens // 8, 8, rank), axis=0))
    top = jnp.max(top, axis=0, keepdims=True)

    def expo_step(i, total):
        at = pl.multiple_of(i * SEG, SEG)
        block = jnp.exp(logit_ref[pl.ds(at, SEG), :] - top)
        expo_ref[pl.ds(at, SEG), :] = block.astype(BF)
        return total + jnp.sum(block.reshape(SEG // 8, 8, rank), axis=0)

    steps = len(pieces) * tokens // SEG
    total = lax.fori_loop(0, steps, expo_step, jnp.zeros((8, rank), FL))
    both = jnp.concatenate([src[:, h * pair : (h + 1) * pair] for src in pieces], axis=0)
    return top, jnp.sum(total, axis=0, keepdims=True), dot_tn(expo_ref[...], both)


def stats_early_kernel(plan, pos, *refs):
    pieces, (w_ref, part_ref, stat_ref, logit_ref, expo_ref) = refs[:-5], refs[-5:]
    heads = plan.heads
    stat_ref[2 * heads :, :] = jnp.zeros((STAT_ROWS - 2 * heads, plan.rank), FL)
    floor = jnp.full((1, plan.rank), -jnp.inf, FL)
    for h in range(heads):
        top, total, part = head_part(plan, h, pieces, w_ref, logit_ref, expo_ref, floor)
        stat_ref[h : h + 1, :] = top
        stat_ref[heads + h : heads + h + 1, :] = total
        part_ref[h] = part


def stats_late_kernel(plan, pos, *refs):
    inner, outer, heads, rank, rows = plan.inner, plan.outer, plan.heads, plan.rank, plan.rows
    pieces, (w_ref, old_ref, old_stat_ref, first_ref, last_ref), refs = (
        refs[:inner],
        refs[inner : inner + 5],
        refs[inner + 5 :],
    )
    outs, (logit_ref, expo_ref, part_ref) = refs[:outer], refs[outer:]
    for k, src in enumerate(pieces):

        @pl.when(pos[1] == k)
        def _():
            first_ref[...] = src[: plan.margin, :]

        @pl.when((pos[1] ^ k) == inner - 1)
        def _():
            last_ref[...] = src[plan.tokens - plan.margin :, :]

    same = lax.broadcasted_iota(jnp.int32, (rank, rank), 0) == lax.broadcasted_iota(
        jnp.int32, (rank, rank), 1
    )
    tops, totals = [], []
    for h in range(heads):
        old_top = old_stat_ref[h : h + 1, :]
        top, total, part = head_part(
            plan, h, pieces[late_from(inner) :], w_ref, logit_ref, expo_ref, old_top
        )
        weight = jnp.exp(old_top - top)
        tops.append(top)
        totals.append(total + weight * old_stat_ref[heads + h : heads + h + 1, :])
        part_ref[h] = part + old_ref[h] * column_of(same, weight)
    stats = jnp.concatenate(
        tops + totals + [jnp.zeros((STAT_ROWS - 2 * heads, rank), FL)], axis=0
    )
    for k, out in enumerate(outs):
        row = pl.multiple_of((pos[0] ^ k) * rows, rows)
        for h in range(heads):
            out[h * rows : (h + 1) * rows, :] = part_ref[h, pl.ds(row, rows), :]
        out[heads * rows :, :] = stats


def late_from(inner):
    return inner // 2 + 1


def own_columns(plan, pos):
    row_at = lax.broadcasted_iota(jnp.int32, (plan.rows, plan.rank), 0)
    col_at = lax.broadcasted_iota(jnp.int32, (plan.rows, plan.rank), 1)
    return col_at == row_at + pos[0] * plan.rows


def combine_kernel(plan, pos, *refs):
    ins, (full_ref, half_ref, stat_ref) = refs[: plan.outer], refs[plan.outer :]
    heads, rows = plan.heads, plan.rows
    own = own_columns(plan, pos)
    stats = [r[heads * rows :, :] for r in ins]
    stat_ref[2 * heads :, :] = jnp.zeros((STAT_ROWS - 2 * heads, plan.rank), FL)
    for h in range(heads):
        tops = [stat[h : h + 1, :] for stat in stats]
        top = tops[0]
        for t in tops[1:]:
            top = jnp.maximum(top, t)
        weights = [jnp.exp(t - top) for t in tops]
        total = weights[0] * stats[0][heads + h : heads + h + 1, :]
        for w, stat in zip(weights[1:], stats[1:]):
            total = total + w * stat[heads + h : heads + h + 1, :]
        inverse = 1.0 / total
        stat_ref[h : h + 1, :] = top
        stat_ref[heads + h : heads + h + 1, :] = inverse
        here = slice(h * rows, (h + 1) * rows)
        result = ins[0][here, :] * column_of(own, weights[0])
        for w, r in zip(weights[1:], ins[1:]):
            result = result + r[here, :] * column_of(own, w)
        result = result * column_of(own, inverse)
        full_ref[here, :] = result
        half_ref[here, :] = result.astype(BF)


def attend_kernel(plan, total_groups, pos, *refs):
    outer, inner, heads = plan.outer, plan.inner, plan.heads
    kv_refs, (before_ref, after_ref), refs = refs[:inner], refs[inner : inner + 2], refs[inner + 2 :]
    bars, qg, refs = refs[:outer], refs[outer : outer + inner], refs[outer + inner :]
    dq_outs, bar_outs, refs = refs[:inner], refs[inner : inner + outer], refs[inner + outer :]
    acc_ref, wg_before_ref, wg_after_ref, ext_ref, bar_ref, q_ref, dbar_ref, dq_ref = refs
    hd, pair, rank, margin, group = plan.head_size, plan.pair, plan.rank, plan.margin, plan.group
    rows = plan.rows
    ext_ref[:margin, :] = before_ref[...]
    for k, src in enumerate(kv_refs):
        row = pl.multiple_of((pos[1] ^ k) * plan.tokens + margin, margin)
        ext_ref[pl.ds(row, plan.tokens), :] = src[...]
    ext_ref[margin + group :, :] = after_ref[...]
    for k, src in enumerate(bars):
        row = pl.multiple_of((pos[0] ^ k) * rows, rows)
        for h in range(heads):
            bar_ref[h, pl.ds(row, rows), :] = src[h * rows : (h + 1) * rows, :]
    for k, src in enumerate(qg):
        row = pl.multiple_of((pos[1] ^ k) * plan.tokens, plan.tokens)
        q_ref[pl.ds(row, plan.tokens), :] = src[...]
    acc_ref[:SEG, :] = jnp.zeros((SEG, plan.width), FL)
    dbar_ref[...] = jnp.zeros(dbar_ref.shape, FL)
    segs = group // SEG
    at_start = pos[0] == 0
    at_end = pos[0] == total_groups - 1
    factor = plan.scale / math.log(2.0)

    def step(j, carry):
        row = pl.multiple_of(j * SEG, SEG)
        hide_low = jnp.where(jnp.logical_and(at_start, j == 0), HIDDEN, 0.0)
        hide_high = jnp.where(jnp.logical_and(at_end, j == segs - 1), HIDDEN, 0.0)
        loaded, scored = [], []
        for h in range(heads):
            low, mid, high = h * pair, h * pair + hd, (h + 1) * pair
            key = jnp.concatenate([bar_ref[h, :, :hd], ext_ref[pl.ds(row, 2 * SEG), low:mid]], axis=0)
            val = jnp.concatenate([bar_ref[h, :, hd:], ext_ref[pl.ds(row, 2 * SEG), mid:high]], axis=0)
            query = q_ref[pl.ds(row, SEG), low:mid]
            grad = q_ref[pl.ds(row, SEG), mid:high]
            loaded.append((key, query, grad))
            scored.append((dot_nt(key, query), dot_nt(val, grad)))
        for h in range(heads):
            low, mid, high = h * pair, h * pair + hd, (h + 1) * pair
            key, query, grad = loaded[h]
            scores, dprob = scored[h]
            scores = jnp.concatenate(
                [
                    scores[:rank],
                    scores[rank : rank + margin] + hide_low,
                    scores[rank + margin : rank + 2 * SEG - margin],
                    scores[rank + 2 * SEG - margin :] + hide_high,
                ],
                axis=0,
            )
            expo = jnp.exp2((scores - jnp.max(scores, axis=0, keepdims=True)) * factor)
            prob = expo * (1.0 / jnp.sum(expo, axis=0, keepdims=True))
            prob_b = prob.astype(BF)
            row_dot = jnp.sum(prob_b.astype(FL) * dprob, axis=0, keepdims=True)
            dscore = (prob * (dprob - row_dot)).astype(BF)
            dquery = dot_tn(key, dscore) * plan.scale
            dq_ref[pl.ds(row, SEG), h * hd : (h + 1) * hd] = jnp.transpose(dquery).astype(BF)
            dkey = dot_nn(dscore, query)
            dval = dot_nn(prob_b, grad)
            dbar_ref[h, :, :hd] += dkey[:rank, :]
            dbar_ref[h, :, hd:] += dval[:rank, :]
            new = pl.multiple_of(row + SEG, SEG)
            acc_ref[pl.ds(row, SEG), low:mid] += dkey[rank : rank + SEG, :]
            acc_ref[pl.ds(row, SEG), mid:high] += dval[rank : rank + SEG, :]
            acc_ref[pl.ds(new, SEG), low:mid] = dkey[rank + SEG :, :]
            acc_ref[pl.ds(new, SEG), mid:high] = dval[rank + SEG :, :]
        return carry

    lax.fori_loop(0, segs, step, 0)
    for h in range(heads):
        low, mid, high = h * pair, h * pair + hd, (h + 1) * pair
        dbar_ref[h, :, :hd] = dbar_ref[h, :, :hd] * plan.scale
        wg_before_ref[:, low:mid] = (acc_ref[:margin, low:mid] * plan.scale).astype(BF)
        wg_before_ref[:, mid:high] = acc_ref[:margin, mid:high].astype(BF)
        wg_after_ref[:, low:mid] = (acc_ref[margin + group :, low:mid] * plan.scale).astype(BF)
        wg_after_ref[:, mid:high] = acc_ref[margin + group :, mid:high].astype(BF)
    for k, out in enumerate(dq_outs):
        row = pl.multiple_of((pos[1] ^ k) * plan.tokens, plan.tokens)
        out[...] = dq_ref[pl.ds(row, plan.tokens), :]
    for k, out in enumerate(bar_outs):
        row = pl.multiple_of((pos[0] ^ k) * rows, rows)
        for h in range(heads):
            out[h * rows : (h + 1) * rows, :] = dbar_ref[h, pl.ds(row, rows), :].astype(BF)


def combine_grad_kernel(plan, pos, *refs):
    full_ref, ins = refs[0], refs[1 : 1 + plan.outer]
    out_ref = refs[1 + plan.outer]
    heads, rows = plan.heads, plan.rows
    total = ins[0][...].astype(FL)
    for r in ins[1:]:
        total = total + r[...].astype(FL)
    half = total.astype(BF)
    out_ref[: heads * rows, :] = half
    column = jnp.sum(full_ref[...] * half.astype(FL), axis=1, keepdims=True)
    own = own_columns(plan, pos)
    parts = []
    for h in range(heads):
        rest = jnp.sum(jnp.where(own, column[h * rows : (h + 1) * rows, :], 0.0), axis=0, keepdims=True)
        for _ in range(3):
            part = rest.astype(BF).astype(FL)
            parts.append(part)
            rest = rest - part
    parts.append(jnp.zeros((DOT_ROWS - 3 * heads, plan.rank), FL))
    out_ref[heads * rows :, :] = jnp.concatenate(parts, axis=0).astype(BF)


def finish_kernel(plan, wave, pos, *refs):
    outer, heads, count = plan.outer, plan.heads, len(wave)
    kv_refs, refs = refs[:count], refs[count:]
    w_ref, stat_ref, wg_ref, before_ref, after_ref = refs[:5]
    bars, refs = refs[5 : 5 + outer], refs[5 + outer :]
    outs, (logit_grad_ref, bar_ref, sum_ref) = refs[:count], refs[count:]
    hd, pair, rank, margin, rows = plan.head_size, plan.pair, plan.rank, plan.margin, plan.rows
    dots = [jnp.zeros((1, rank), FL)] * heads
    for k, src in enumerate(bars):
        row = pl.multiple_of((pos[0] ^ k) * rows, rows)
        sent = src[heads * rows :, :].astype(FL)
        for h in range(heads):
            bar_ref[h, pl.ds(row, rows), :] = src[h * rows : (h + 1) * rows, :]
            dots[h] = dots[h] + jnp.sum(sent[3 * h : 3 * h + 3, :], axis=0, keepdims=True)
    subs = plan.tokens // SEG
    for i, k in enumerate(wave):
        piece_at = pos[1] ^ k
        for sub in range(subs):
            here = slice(sub * SEG, (sub + 1) * SEG)
            from_row = pl.multiple_of(piece_at * plan.tokens + sub * SEG + margin, margin)
            for h in range(heads):
                low, mid, high = h * pair, h * pair + hd, (h + 1) * pair
                both = kv_refs[i][here, low:high]
                dbar = bar_ref[h]
                top = stat_ref[h : h + 1, :]
                inverse = stat_ref[heads + h : heads + h + 1, :]
                expo = jnp.exp(dot_nn(both[:, :hd], w_ref[h]) - top).astype(BF).astype(FL)
                prob = expo * inverse
                dprob = dot_nt(both, dbar)
                logit_grad = (prob * (dprob - dots[h])).astype(BF)
                lines = slice(i * plan.tokens + sub * SEG, i * plan.tokens + (sub + 1) * SEG)
                logit_grad_ref[lines, h * rank : (h + 1) * rank] = logit_grad
                from_prob = dot_nn(prob.astype(BF), dbar)
                window_key = wg_ref[pl.ds(from_row, SEG), low:mid] * plan.scale
                sum_ref[h, :, :hd] = from_prob[:, :hd] + window_key + dot_nt(logit_grad, w_ref[h])
                sum_ref[h, :, hd:] = from_prob[:, hd:] + wg_ref[pl.ds(from_row, SEG), mid:high]
            if sub == 0:

                @pl.when(piece_at == 0)
                def _():
                    for h in range(heads):
                        edge = before_ref[:, h * pair : (h + 1) * pair]
                        sum_ref[h, :margin, :] += edge.astype(FL)

            if sub == subs - 1:

                @pl.when(piece_at == plan.inner - 1)
                def _():
                    for h in range(heads):
                        edge = after_ref[:, h * pair : (h + 1) * pair]
                        sum_ref[h, SEG - margin :, :] += edge.astype(FL)

            for h in range(heads):
                outs[i][here, h * pair : (h + 1) * pair] = sum_ref[h].astype(BF)


def proj_kernel(plan, waves, pos, *refs):
    heads, hd, pair, rank = plan.heads, plan.head_size, plan.pair, plan.rank
    kv_refs, refs = refs[: plan.inner], refs[plan.inner :]
    grad_refs, refs = refs[: len(waves)], refs[len(waves) :]
    outs, proj_ref = refs[: plan.outer], refs[plan.outer]
    for h in range(heads):
        total = jnp.zeros((hd, rank), FL)
        for wave, grad_ref in zip(waves, grad_refs):
            key = jnp.concatenate([kv_refs[k][:, h * pair : h * pair + hd] for k in wave], axis=0)
            total = total + dot_tn(key, grad_ref[:, h * rank : (h + 1) * rank])
        proj_ref[h * hd : (h + 1) * hd, :] = total
    piece = heads * hd // plan.outer
    for k, out in enumerate(outs):
        row = pl.multiple_of((pos[0] ^ k) * piece, piece)
        out[...] = proj_ref[pl.ds(row, piece), :]


def finish_waves(inner):
    quarter = inner // 4
    return (
        tuple(range(inner - quarter, inner)),
        tuple(range(quarter, inner - quarter)),
        tuple(range(quarter)),
    )


def put(items, which, values):
    for k, value in zip(which, values):
        items[k] = value


def exchange(fields, devices, stride, which=None):
    out = []
    for k, field in zip(which or range(len(fields)), fields):
        flip = [(i, i ^ (k * stride)) for i in range(devices)]
        out.append(lax.ppermute(field, "seq", flip) if k else field)
    return out


def swap_edges(upward, downward, devices, stride):
    up = [(i, i + stride) for i in range(devices - stride)]
    down = [(j, i) for i, j in up]
    return lax.ppermute(upward, "seq", up), lax.ppermute(downward, "seq", down)


def per_device(queries, keys, values, grad_out, proj_weight):
    tokens_here, row_width = queries.shape
    head_count, head_size, rank = proj_weight.shape
    devices = lax.axis_size("seq")
    plan = Plan(devices, tokens_here, head_count, head_size, rank)
    inner, outer, heads = plan.inner, plan.outer, plan.heads
    group, width, rows, margin = plan.group, plan.width, plan.rows, plan.margin
    me = lax.axis_index("seq")
    pos = jnp.stack([me // inner, me % inner]).astype(jnp.int32)

    def bind(kernel, *more):
        return lambda pos_ref, *refs: kernel(plan, *more, pos_ref, *refs)

    weight = lax.dynamic_slice_in_dim(proj_weight, (me % inner) * heads, heads, axis=0)
    pair = plan.pair
    piece = struct((tokens_here, width), BF)

    waves = finish_waves(inner)

    def pack(first, second):
        return call(
            bind(pack_kernel),
            pos,
            [first, second],
            [piece] * inner,
            [
                pltpu.SemaphoreType.DMA((2 * inner * heads,)),
                pltpu.SemaphoreType.DMA((inner,)),
                pltpu.VMEM((inner, tokens_here, width), BF),
            ],
            far="ins outs",
        )

    kv_pieces = exchange(pack(keys, values), devices, 1)
    qg_pieces = exchange(pack(queries, grad_out), devices, 1)

    early = late_from(inner)
    old_part, old_stat = call(
        bind(stats_early_kernel),
        pos,
        [*kv_pieces[:early], weight],
        [struct((heads, rank, pair), FL), struct((STAT_ROWS, rank), FL)],
        [pltpu.VMEM((early * tokens_here, rank), FL), pltpu.VMEM((early * tokens_here, rank), BF)],
    )
    late = inner - early
    kv_first, kv_last, *part_send = call(
        bind(stats_late_kernel),
        pos,
        [*kv_pieces, weight, old_part, old_stat],
        [struct((margin, width), BF)] * 2
        + [struct((heads * rows + STAT_ROWS, pair), FL)] * outer,
        [
            pltpu.VMEM((late * tokens_here, rank), FL),
            pltpu.VMEM((late * tokens_here, rank), BF),
            pltpu.VMEM((heads, rank, pair), FL),
        ],
    )
    parts = exchange(part_send, devices, inner)
    kv_before, kv_after = swap_edges(kv_last, kv_first, devices, inner)
    bar_full, bar_half, stats = call(
        bind(combine_kernel),
        pos,
        parts,
        [
            struct((heads * rows, pair), FL),
            struct((heads * rows, pair), BF),
            struct((STAT_ROWS, rank), FL),
        ],
    )
    bars = exchange([bar_half] * outer, devices, inner)

    edge = struct((margin, width), BF)
    results = call(
        bind(attend_kernel, outer),
        pos,
        [*kv_pieces, kv_before, kv_after, *bars, *qg_pieces],
        [struct((tokens_here, heads * head_size), BF)] * inner
        + [struct((heads * rows, pair), BF)] * outer
        + [struct((group + 2 * margin, width), FL), edge, edge],
        [
            pltpu.VMEM((group + 2 * margin, width), BF),
            pltpu.VMEM((heads, rank, pair), BF),
            pltpu.VMEM((group, width), BF),
            pltpu.VMEM((heads, rank, pair), FL),
            pltpu.VMEM((group, heads * head_size), BF),
        ],
    )
    dq_send = results[:inner]
    dbar_send = results[inner : inner + outer]
    wg, wg_before, wg_after = results[inner + outer :]
    dbar_parts = exchange(dbar_send, devices, inner)
    wg_from_before, wg_from_after = swap_edges(wg_after, wg_before, devices, inner)
    (dbar_half,) = call(
        bind(combine_grad_kernel),
        pos,
        [bar_full, *dbar_parts],
        [struct((heads * rows + DOT_ROWS, pair), BF)],
    )
    dbars = exchange([dbar_half] * outer, devices, inner)
    dq_pieces = [None] * inner
    first, others = waves[0], tuple(k for k in range(inner) if k not in waves[0])
    put(dq_pieces, first, exchange([dq_send[k] for k in first], devices, 1, first))
    put(dq_pieces, others, exchange([dq_send[k] for k in others], devices, 1, others))

    dkv_pieces, logit_grads = [None] * inner, []
    for wave in waves:
        *dkv_send, logit_grad = call(
            bind(finish_kernel, wave),
            pos,
            [*(kv_pieces[k] for k in wave), weight, stats, wg, wg_from_before, wg_from_after, *dbars],
            [piece] * len(wave) + [struct((len(wave) * tokens_here, heads * rank), BF)],
            [pltpu.VMEM((heads, rank, pair), BF), pltpu.VMEM((heads, SEG, pair), FL)],
        )
        logit_grads.append(logit_grad)
        put(dkv_pieces, wave, exchange(dkv_send, devices, 1, wave))
    proj_send = call(
        bind(proj_kernel, waves),
        pos,
        [*kv_pieces, *logit_grads],
        [struct((heads * head_size // outer, rank), FL)] * outer,
        [pltpu.VMEM((heads * head_size, rank), FL)],
    )
    proj_parts = exchange(proj_send, devices, inner)
    proj_sum = proj_parts[0]
    for part in proj_parts[1:]:
        proj_sum = proj_sum + part
    place = [(o * inner + p, p * outer + o) for o in range(outer) for p in range(inner)]
    proj_here = lax.ppermute(proj_sum, "seq", place)
    whole = struct((tokens_here, row_width), BF)
    (grad_queries,) = call(
        bind(unpack_kernel), pos, dq_pieces, [whole], [pltpu.SemaphoreType.DMA((inner,))], far="outs"
    )
    sooner, later = waves[2] + waves[0], waves[1]
    grads = call(
        bind(unpack_pair_kernel, sooner, False),
        pos,
        [dkv_pieces[k] for k in sooner],
        [whole, whole],
        [pltpu.SemaphoreType.DMA((2 * len(sooner) * heads,))],
        far="outs",
    )
    count = len(later)
    grad_keys, grad_values, grad_proj = call(
        bind(unpack_pair_kernel, later, True),
        pos,
        [*(dkv_pieces[k] for k in later), proj_here, *grads],
        [whole, whole, struct(proj_here.shape, FL)],
        [pltpu.SemaphoreType.DMA((2 * count * heads + 1,))],
        far="outs",
        aliases=((count + 1, 0), (count + 2, 1)),
    )
    return (grad_queries, grad_keys, grad_values, grad_proj)


def solution(mesh):
    in_specs = (P("seq", None), P("seq", None), P("seq", None), P("seq", None), P())
    out_specs = (P("seq", None), P("seq", None), P("seq", None), P("seq", None))
    return jax.shard_map(
        per_device, mesh=mesh, in_specs=in_specs, out_specs=out_specs, check_vma=False
    )
```

```python
import math

import jax
import jax.numpy as jnp
from jax import lax
from jax.experimental import pallas as pl
from jax.experimental.pallas import tpu as pltpu
from jax.sharding import PartitionSpec as P


SEG = 256
STAT_ROWS = 8
DOT_ROWS = 16
HIDDEN = -1e30
HEADS_PER_DEVICE = 2
BF = jnp.bfloat16
FL = jnp.float32


def dot_nn(a, b):
    return lax.dot_general(a, b, (((1,), (0,)), ((), ())), preferred_element_type=FL)


def dot_nt(a, b):
    return lax.dot_general(a, b, (((1,), (1,)), ((), ())), preferred_element_type=FL)


def dot_tn(a, b):
    return lax.dot_general(a, b, (((0,), (0,)), ((), ())), preferred_element_type=FL)


def struct(shape, dtype):
    return jax.ShapeDtypeStruct(shape, dtype)


def size_of(x):
    dtype = jnp.dtype(x.dtype)
    return math.prod(x.shape) * dtype.itemsize


def call(kernel, pos, ins, outs, scratch=(), spare=4, far="", aliases=()):
    near = pl.BlockSpec(memory_space=pltpu.VMEM)
    hbm = pl.BlockSpec(memory_space=pltpu.HBM)
    held = [x for x in scratch if hasattr(x.dtype, "itemsize")]
    if "ins" in far:
        ins = [pltpu.with_memory_space_constraint(x, pltpu.HBM) for x in ins]
    else:
        held += [x for i, x in enumerate(ins) if i not in dict(aliases)]
    if "outs" not in far:
        held += outs
    return pl.pallas_call(
        kernel,
        in_specs=[pl.BlockSpec(memory_space=pltpu.SMEM)]
        + [hbm if "ins" in far or i in dict(aliases) else near for i in range(len(ins))],
        out_specs=[hbm if "outs" in far else near] * len(outs),
        out_shape=list(outs),
        scratch_shapes=list(scratch),
        input_output_aliases={i + 1: o for i, o in aliases},
        compiler_params=pltpu.CompilerParams(
            vmem_limit_bytes=sum(map(size_of, held)) + spare * 2**20
        ),
    )(pos, *ins)


class Plan:
    def __init__(self, devices, tokens_here, head_count, head_size, rank):
        self.inner = math.gcd(head_count // HEADS_PER_DEVICE, devices)
        self.outer = devices // self.inner
        self.heads = head_count // self.inner
        self.devices = devices
        self.tokens = tokens_here
        self.group = tokens_here * self.inner
        self.head_size = head_size
        self.rank = rank
        self.pair = 2 * head_size
        self.width = self.heads * self.pair
        self.rows = rank // self.outer
        self.margin = SEG // 2
        self.scale = head_size ** (-0.5)


def run_copies(sems, moves):
    copies = [pltpu.make_async_copy(a, b, sems.at[i]) for i, (a, b) in enumerate(moves)]
    for copy in copies:
        copy.start()
    for copy in copies:
        copy.wait()


def head_slices(plan, other, h):
    return pl.ds(pl.multiple_of((other * plan.heads + h) * plan.head_size, plan.head_size), plan.head_size)


def pack_kernel(plan, pos, a_ref, b_ref, *refs):
    outs, (in_sems, out_sems, buffer) = refs[: plan.inner], refs[plan.inner :]
    hd = plan.head_size
    coming, leaving = [], []
    for k, out in enumerate(outs):
        for h in range(plan.heads):
            cols = head_slices(plan, pos[1] ^ k, h)
            for side, src in enumerate((a_ref, b_ref)):
                at = 2 * h + side
                coming.append(
                    pltpu.make_async_copy(
                        src.at[:, cols],
                        buffer.at[k, :, pl.ds(at * hd, hd)],
                        in_sems.at[2 * plan.heads * k + at],
                    )
                )
        leaving.append(pltpu.make_async_copy(buffer.at[k], out, out_sems.at[k]))
    for copy in coming:
        copy.start()
    for k in range(plan.inner):
        for copy in coming[2 * plan.heads * k : 2 * plan.heads * (k + 1)]:
            copy.wait()
        leaving[k].start()
    for copy in leaving:
        copy.wait()


def unpack_pair_kernel(plan, which, last, pos, *refs):
    ins, refs = refs[: len(which)], refs[len(which) :]
    moves = []
    if last:
        parts, (_, _, a_ref, b_ref, out_ref, sems, sum_ref) = refs[: plan.outer], refs[plan.outer :]
        total = parts[0][...]
        for part in parts[1:]:
            total = total + part[...]
        sum_ref[...] = total
        moves.append((sum_ref, out_ref))
    else:
        a_ref, b_ref, sems = refs
    hd = plan.head_size
    for k, src in zip(which, ins):
        for h in range(plan.heads):
            cols = head_slices(plan, pos[1] ^ k, h)
            moves.append((src.at[:, pl.ds(2 * h * hd, hd)], a_ref.at[:, cols]))
            moves.append((src.at[:, pl.ds((2 * h + 1) * hd, hd)], b_ref.at[:, cols]))
    run_copies(sems, moves)


def unpack_kernel(plan, pos, *refs):
    ins, a_ref, sems = refs[: plan.inner], refs[plan.inner], refs[plan.inner + 1]
    wide = plan.heads * plan.head_size
    moves = []
    for k, src in enumerate(ins):
        cols = pl.ds(pl.multiple_of((pos[1] ^ k) * wide, wide), wide)
        moves.append((src, a_ref.at[:, cols]))
    run_copies(sems, moves)


def column_of(mask, row):
    return jnp.sum(jnp.where(mask, row, 0.0), axis=1, keepdims=True)


def head_part(plan, h, pieces, w_ref, logit_ref, expo_ref, floor):
    hd, pair, rank, tokens = plan.head_size, plan.pair, plan.rank, plan.tokens
    top = jnp.broadcast_to(floor, (8, rank))
    for i, src in enumerate(pieces):
        block = dot_nn(src[:, h * pair : h * pair + hd], w_ref[h])
        logit_ref[i * tokens : (i + 1) * tokens, :] = block
        top = jnp.maximum(top, jnp.max(block.reshape(tokens // 8, 8, rank), axis=0))
    top = jnp.max(top, axis=0, keepdims=True)

    def expo_step(i, total):
        at = pl.multiple_of(i * SEG, SEG)
        block = jnp.exp(logit_ref[pl.ds(at, SEG), :] - top)
        expo_ref[pl.ds(at, SEG), :] = block.astype(BF)
        return total + jnp.sum(block.reshape(SEG // 8, 8, rank), axis=0)

    steps = len(pieces) * tokens // SEG
    total = lax.fori_loop(0, steps, expo_step, jnp.zeros((8, rank), FL))
    both = jnp.concatenate([src[:, h * pair : (h + 1) * pair] for src in pieces], axis=0)
    return top, jnp.sum(total, axis=0, keepdims=True), dot_tn(expo_ref[...], both)


def stats_early_kernel(plan, pos, *refs):
    pieces, (w_ref, part_ref, stat_ref, logit_ref, expo_ref) = refs[:-5], refs[-5:]
    heads = plan.heads
    stat_ref[2 * heads :, :] = jnp.zeros((STAT_ROWS - 2 * heads, plan.rank), FL)
    floor = jnp.full((1, plan.rank), -jnp.inf, FL)
    for h in range(heads):
        top, total, part = head_part(plan, h, pieces, w_ref, logit_ref, expo_ref, floor)
        stat_ref[h : h + 1, :] = top
        stat_ref[heads + h : heads + h + 1, :] = total
        part_ref[h] = part


def stats_late_kernel(plan, pos, *refs):
    inner, outer, heads, rank, rows = plan.inner, plan.outer, plan.heads, plan.rank, plan.rows
    pieces, (w_ref, old_ref, old_stat_ref, first_ref, last_ref), refs = (
        refs[:inner],
        refs[inner : inner + 5],
        refs[inner + 5 :],
    )
    outs, (logit_ref, expo_ref, part_ref) = refs[:outer], refs[outer:]
    for k, src in enumerate(pieces):

        @pl.when(pos[1] == k)
        def _():
            first_ref[...] = src[: plan.margin, :]

        @pl.when((pos[1] ^ k) == inner - 1)
        def _():
            last_ref[...] = src[plan.tokens - plan.margin :, :]

    same = lax.broadcasted_iota(jnp.int32, (rank, rank), 0) == lax.broadcasted_iota(
        jnp.int32, (rank, rank), 1
    )
    tops, totals = [], []
    for h in range(heads):
        old_top = old_stat_ref[h : h + 1, :]
        top, total, part = head_part(
            plan, h, pieces[late_from(inner) :], w_ref, logit_ref, expo_ref, old_top
        )
        weight = jnp.exp(old_top - top)
        tops.append(top)
        totals.append(total + weight * old_stat_ref[heads + h : heads + h + 1, :])
        part_ref[h] = part + old_ref[h] * column_of(same, weight)
    stats = jnp.concatenate(
        tops + totals + [jnp.zeros((STAT_ROWS - 2 * heads, rank), FL)], axis=0
    )
    for k, out in enumerate(outs):
        row = pl.multiple_of((pos[0] ^ k) * rows, rows)
        for h in range(heads):
            out[h * rows : (h + 1) * rows, :] = part_ref[h, pl.ds(row, rows), :]
        out[heads * rows :, :] = stats


def late_from(inner):
    return inner // 2 + 1


def own_columns(plan, pos):
    row_at = lax.broadcasted_iota(jnp.int32, (plan.rows, plan.rank), 0)
    col_at = lax.broadcasted_iota(jnp.int32, (plan.rows, plan.rank), 1)
    return col_at == row_at + pos[0] * plan.rows


def combine_kernel(plan, pos, *refs):
    ins, (full_ref, half_ref, stat_ref) = refs[: plan.outer], refs[plan.outer :]
    heads, rows = plan.heads, plan.rows
    own = own_columns(plan, pos)
    stats = [r[heads * rows :, :] for r in ins]
    stat_ref[2 * heads :, :] = jnp.zeros((STAT_ROWS - 2 * heads, plan.rank), FL)
    for h in range(heads):
        tops = [stat[h : h + 1, :] for stat in stats]
        top = tops[0]
        for t in tops[1:]:
            top = jnp.maximum(top, t)
        weights = [jnp.exp(t - top) for t in tops]
        total = weights[0] * stats[0][heads + h : heads + h + 1, :]
        for w, stat in zip(weights[1:], stats[1:]):
            total = total + w * stat[heads + h : heads + h + 1, :]
        inverse = 1.0 / total
        stat_ref[h : h + 1, :] = top
        stat_ref[heads + h : heads + h + 1, :] = inverse
        here = slice(h * rows, (h + 1) * rows)
        result = ins[0][here, :] * column_of(own, weights[0])
        for w, r in zip(weights[1:], ins[1:]):
            result = result + r[here, :] * column_of(own, w)
        result = result * column_of(own, inverse)
        full_ref[here, :] = result
        half_ref[here, :] = result.astype(BF)


def attend_kernel(plan, total_groups, pos, *refs):
    outer, inner, heads = plan.outer, plan.inner, plan.heads
    kv_refs, (before_ref, after_ref), refs = refs[:inner], refs[inner : inner + 2], refs[inner + 2 :]
    bars, qg, refs = refs[:outer], refs[outer : outer + inner], refs[outer + inner :]
    dq_outs, bar_outs, refs = refs[:inner], refs[inner : inner + outer], refs[inner + outer :]
    acc_ref, wg_before_ref, wg_after_ref, ext_ref, bar_ref, q_ref, dbar_ref, dq_ref = refs
    hd, pair, rank, margin, group = plan.head_size, plan.pair, plan.rank, plan.margin, plan.group
    rows = plan.rows
    ext_ref[:margin, :] = before_ref[...]
    for k, src in enumerate(kv_refs):
        row = pl.multiple_of((pos[1] ^ k) * plan.tokens + margin, margin)
        ext_ref[pl.ds(row, plan.tokens), :] = src[...]
    ext_ref[margin + group :, :] = after_ref[...]
    for k, src in enumerate(bars):
        row = pl.multiple_of((pos[0] ^ k) * rows, rows)
        for h in range(heads):
            bar_ref[h, pl.ds(row, rows), :] = src[h * rows : (h + 1) * rows, :]
    for k, src in enumerate(qg):
        row = pl.multiple_of((pos[1] ^ k) * plan.tokens, plan.tokens)
        q_ref[pl.ds(row, plan.tokens), :] = src[...]
    acc_ref[:SEG, :] = jnp.zeros((SEG, plan.width), FL)
    dbar_ref[...] = jnp.zeros(dbar_ref.shape, FL)
    segs = group // SEG
    at_start = pos[0] == 0
    at_end = pos[0] == total_groups - 1
    factor = plan.scale / math.log(2.0)

    def step(j, carry):
        row = pl.multiple_of(j * SEG, SEG)
        hide_low = jnp.where(jnp.logical_and(at_start, j == 0), HIDDEN, 0.0)
        hide_high = jnp.where(jnp.logical_and(at_end, j == segs - 1), HIDDEN, 0.0)
        loaded, scored = [], []
        for h in range(heads):
            low, mid, high = h * pair, h * pair + hd, (h + 1) * pair
            key = jnp.concatenate([bar_ref[h, :, :hd], ext_ref[pl.ds(row, 2 * SEG), low:mid]], axis=0)
            val = jnp.concatenate([bar_ref[h, :, hd:], ext_ref[pl.ds(row, 2 * SEG), mid:high]], axis=0)
            query = q_ref[pl.ds(row, SEG), low:mid]
            grad = q_ref[pl.ds(row, SEG), mid:high]
            loaded.append((key, query, grad))
            scored.append((dot_nt(key, query), dot_nt(val, grad)))
        for h in range(heads):
            low, mid, high = h * pair, h * pair + hd, (h + 1) * pair
            key, query, grad = loaded[h]
            scores, dprob = scored[h]
            scores = jnp.concatenate(
                [
                    scores[:rank],
                    scores[rank : rank + margin] + hide_low,
                    scores[rank + margin : rank + 2 * SEG - margin],
                    scores[rank + 2 * SEG - margin :] + hide_high,
                ],
                axis=0,
            )
            expo = jnp.exp2((scores - jnp.max(scores, axis=0, keepdims=True)) * factor)
            prob = expo * (1.0 / jnp.sum(expo, axis=0, keepdims=True))
            prob_b = prob.astype(BF)
            row_dot = jnp.sum(prob_b.astype(FL) * dprob, axis=0, keepdims=True)
            dscore = (prob * (dprob - row_dot)).astype(BF)
            dquery = dot_tn(key, dscore) * plan.scale
            dq_ref[pl.ds(row, SEG), h * hd : (h + 1) * hd] = jnp.transpose(dquery).astype(BF)
            dkey = dot_nn(dscore, query)
            dval = dot_nn(prob_b, grad)
            dbar_ref[h, :, :hd] += dkey[:rank, :]
            dbar_ref[h, :, hd:] += dval[:rank, :]
            new = pl.multiple_of(row + SEG, SEG)
            acc_ref[pl.ds(row, SEG), low:mid] += dkey[rank : rank + SEG, :]
            acc_ref[pl.ds(row, SEG), mid:high] += dval[rank : rank + SEG, :]
            acc_ref[pl.ds(new, SEG), low:mid] = dkey[rank + SEG :, :]
            acc_ref[pl.ds(new, SEG), mid:high] = dval[rank + SEG :, :]
        return carry

    lax.fori_loop(0, segs, step, 0)
    for h in range(heads):
        low, mid, high = h * pair, h * pair + hd, (h + 1) * pair
        dbar_ref[h, :, :hd] = dbar_ref[h, :, :hd] * plan.scale
        wg_before_ref[:, low:mid] = (acc_ref[:margin, low:mid] * plan.scale).astype(BF)
        wg_before_ref[:, mid:high] = acc_ref[:margin, mid:high].astype(BF)
        wg_after_ref[:, low:mid] = (acc_ref[margin + group :, low:mid] * plan.scale).astype(BF)
        wg_after_ref[:, mid:high] = acc_ref[margin + group :, mid:high].astype(BF)
    for k, out in enumerate(dq_outs):
        row = pl.multiple_of((pos[1] ^ k) * plan.tokens, plan.tokens)
        out[...] = dq_ref[pl.ds(row, plan.tokens), :]
    for k, out in enumerate(bar_outs):
        row = pl.multiple_of((pos[0] ^ k) * rows, rows)
        for h in range(heads):
            out[h * rows : (h + 1) * rows, :] = dbar_ref[h, pl.ds(row, rows), :].astype(BF)


def combine_grad_kernel(plan, pos, *refs):
    full_ref, ins = refs[0], refs[1 : 1 + plan.outer]
    out_ref = refs[1 + plan.outer]
    heads, rows = plan.heads, plan.rows
    total = ins[0][...].astype(FL)
    for r in ins[1:]:
        total = total + r[...].astype(FL)
    half = total.astype(BF)
    out_ref[: heads * rows, :] = half
    column = jnp.sum(full_ref[...] * half.astype(FL), axis=1, keepdims=True)
    own = own_columns(plan, pos)
    parts = []
    for h in range(heads):
        rest = jnp.sum(jnp.where(own, column[h * rows : (h + 1) * rows, :], 0.0), axis=0, keepdims=True)
        for _ in range(3):
            part = rest.astype(BF).astype(FL)
            parts.append(part)
            rest = rest - part
    parts.append(jnp.zeros((DOT_ROWS - 3 * heads, plan.rank), FL))
    out_ref[heads * rows :, :] = jnp.concatenate(parts, axis=0).astype(BF)


def finish_kernel(plan, wave, pos, *refs):
    outer, heads, count = plan.outer, plan.heads, len(wave)
    kv_refs, refs = refs[:count], refs[count:]
    w_ref, stat_ref, wg_ref, before_ref, after_ref = refs[:5]
    bars, refs = refs[5 : 5 + outer], refs[5 + outer :]
    outs, (logit_grad_ref, bar_ref, sum_ref) = refs[:count], refs[count:]
    hd, pair, rank, margin, rows = plan.head_size, plan.pair, plan.rank, plan.margin, plan.rows
    dots = [jnp.zeros((1, rank), FL)] * heads
    for k, src in enumerate(bars):
        row = pl.multiple_of((pos[0] ^ k) * rows, rows)
        sent = src[heads * rows :, :].astype(FL)
        for h in range(heads):
            bar_ref[h, pl.ds(row, rows), :] = src[h * rows : (h + 1) * rows, :]
            dots[h] = dots[h] + jnp.sum(sent[3 * h : 3 * h + 3, :], axis=0, keepdims=True)
    subs = plan.tokens // SEG
    for i, k in enumerate(wave):
        piece_at = pos[1] ^ k
        for sub in range(subs):
            here = slice(sub * SEG, (sub + 1) * SEG)
            from_row = pl.multiple_of(piece_at * plan.tokens + sub * SEG + margin, margin)
            for h in range(heads):
                low, mid, high = h * pair, h * pair + hd, (h + 1) * pair
                both = kv_refs[i][here, low:high]
                dbar = bar_ref[h]
                top = stat_ref[h : h + 1, :]
                inverse = stat_ref[heads + h : heads + h + 1, :]
                expo = jnp.exp(dot_nn(both[:, :hd], w_ref[h]) - top).astype(BF).astype(FL)
                prob = expo * inverse
                dprob = dot_nt(both, dbar)
                logit_grad = (prob * (dprob - dots[h])).astype(BF)
                lines = slice(i * plan.tokens + sub * SEG, i * plan.tokens + (sub + 1) * SEG)
                logit_grad_ref[lines, h * rank : (h + 1) * rank] = logit_grad
                from_prob = dot_nn(prob.astype(BF), dbar)
                window_key = wg_ref[pl.ds(from_row, SEG), low:mid] * plan.scale
                sum_ref[h, :, :hd] = from_prob[:, :hd] + window_key + dot_nt(logit_grad, w_ref[h])
                sum_ref[h, :, hd:] = from_prob[:, hd:] + wg_ref[pl.ds(from_row, SEG), mid:high]
            if sub == 0:

                @pl.when(piece_at == 0)
                def _():
                    for h in range(heads):
                        edge = before_ref[:, h * pair : (h + 1) * pair]
                        sum_ref[h, :margin, :] += edge.astype(FL)

            if sub == subs - 1:

                @pl.when(piece_at == plan.inner - 1)
                def _():
                    for h in range(heads):
                        edge = after_ref[:, h * pair : (h + 1) * pair]
                        sum_ref[h, SEG - margin :, :] += edge.astype(FL)

            for h in range(heads):
                outs[i][here, h * pair : (h + 1) * pair] = sum_ref[h].astype(BF)


def proj_kernel(plan, waves, pos, *refs):
    heads, hd, pair, rank = plan.heads, plan.head_size, plan.pair, plan.rank
    kv_refs, refs = refs[: plan.inner], refs[plan.inner :]
    grad_refs, refs = refs[: len(waves)], refs[len(waves) :]
    outs, proj_ref = refs[: plan.outer], refs[plan.outer]
    for h in range(heads):
        total = jnp.zeros((hd, rank), FL)
        for wave, grad_ref in zip(waves, grad_refs):
            key = jnp.concatenate([kv_refs[k][:, h * pair : h * pair + hd] for k in wave], axis=0)
            total = total + dot_tn(key, grad_ref[:, h * rank : (h + 1) * rank])
        proj_ref[h * hd : (h + 1) * hd, :] = total
    piece = heads * hd // plan.outer
    for k, out in enumerate(outs):
        row = pl.multiple_of((pos[0] ^ k) * piece, piece)
        out[...] = proj_ref[pl.ds(row, piece), :]


def finish_waves(inner):
    quarter = inner // 4
    return (
        tuple(range(inner - quarter, inner)),
        tuple(range(quarter, inner - quarter)),
        tuple(range(quarter)),
    )


def put(items, which, values):
    for k, value in zip(which, values):
        items[k] = value


def exchange(fields, devices, stride, which=None):
    out = []
    for k, field in zip(which or range(len(fields)), fields):
        flip = [(i, i ^ (k * stride)) for i in range(devices)]
        out.append(lax.ppermute(field, "seq", flip) if k else field)
    return out


def swap_edges(upward, downward, devices, stride):
    up = [(i, i + stride) for i in range(devices - stride)]
    down = [(j, i) for i, j in up]
    return lax.ppermute(upward, "seq", up), lax.ppermute(downward, "seq", down)


def per_device(queries, keys, values, grad_out, proj_weight):
    tokens_here, row_width = queries.shape
    head_count, head_size, rank = proj_weight.shape
    devices = lax.axis_size("seq")
    plan = Plan(devices, tokens_here, head_count, head_size, rank)
    inner, outer, heads = plan.inner, plan.outer, plan.heads
    group, width, rows, margin = plan.group, plan.width, plan.rows, plan.margin
    me = lax.axis_index("seq")
    pos = jnp.stack([me // inner, me % inner]).astype(jnp.int32)

    def bind(kernel, *more):
        return lambda pos_ref, *refs: kernel(plan, *more, pos_ref, *refs)

    weight = lax.dynamic_slice_in_dim(proj_weight, (me % inner) * heads, heads, axis=0)
    pair = plan.pair
    piece = struct((tokens_here, width), BF)

    waves = finish_waves(inner)

    def pack(first, second):
        return call(
            bind(pack_kernel),
            pos,
            [first, second],
            [piece] * inner,
            [
                pltpu.SemaphoreType.DMA((2 * inner * heads,)),
                pltpu.SemaphoreType.DMA((inner,)),
                pltpu.VMEM((inner, tokens_here, width), BF),
            ],
            far="ins outs",
        )

    kv_pieces = exchange(pack(keys, values), devices, 1)
    qg_pieces = exchange(pack(queries, grad_out), devices, 1)

    early = late_from(inner)
    old_part, old_stat = call(
        bind(stats_early_kernel),
        pos,
        [*kv_pieces[:early], weight],
        [struct((heads, rank, pair), FL), struct((STAT_ROWS, rank), FL)],
        [pltpu.VMEM((early * tokens_here, rank), FL), pltpu.VMEM((early * tokens_here, rank), BF)],
    )
    late = inner - early
    kv_first, kv_last, *part_send = call(
        bind(stats_late_kernel),
        pos,
        [*kv_pieces, weight, old_part, old_stat],
        [struct((margin, width), BF)] * 2
        + [struct((heads * rows + STAT_ROWS, pair), FL)] * outer,
        [
            pltpu.VMEM((late * tokens_here, rank), FL),
            pltpu.VMEM((late * tokens_here, rank), BF),
            pltpu.VMEM((heads, rank, pair), FL),
        ],
    )
    parts = exchange(part_send, devices, inner)
    kv_before, kv_after = swap_edges(kv_last, kv_first, devices, inner)
    bar_full, bar_half, stats = call(
        bind(combine_kernel),
        pos,
        parts,
        [
            struct((heads * rows, pair), FL),
            struct((heads * rows, pair), BF),
            struct((STAT_ROWS, rank), FL),
        ],
    )
    bars = exchange([bar_half] * outer, devices, inner)

    edge = struct((margin, width), BF)
    results = call(
        bind(attend_kernel, outer),
        pos,
        [*kv_pieces, kv_before, kv_after, *bars, *qg_pieces],
        [struct((tokens_here, heads * head_size), BF)] * inner
        + [struct((heads * rows, pair), BF)] * outer
        + [struct((group + 2 * margin, width), FL), edge, edge],
        [
            pltpu.VMEM((group + 2 * margin, width), BF),
            pltpu.VMEM((heads, rank, pair), BF),
            pltpu.VMEM((group, width), BF),
            pltpu.VMEM((heads, rank, pair), FL),
            pltpu.VMEM((group, heads * head_size), BF),
        ],
    )
    dq_send = results[:inner]
    dbar_send = results[inner : inner + outer]
    wg, wg_before, wg_after = results[inner + outer :]
    dbar_parts = exchange(dbar_send, devices, inner)
    wg_from_before, wg_from_after = swap_edges(wg_after, wg_before, devices, inner)
    (dbar_half,) = call(
        bind(combine_grad_kernel),
        pos,
        [bar_full, *dbar_parts],
        [struct((heads * rows + DOT_ROWS, pair), BF)],
    )
    dbars = exchange([dbar_half] * outer, devices, inner)
    dq_pieces = [None] * inner
    first, others = waves[0], tuple(k for k in range(inner) if k not in waves[0])
    put(dq_pieces, first, exchange([dq_send[k] for k in first], devices, 1, first))
    put(dq_pieces, others, exchange([dq_send[k] for k in others], devices, 1, others))

    dkv_pieces, logit_grads = [None] * inner, []
    for wave in waves:
        *dkv_send, logit_grad = call(
            bind(finish_kernel, wave),
            pos,
            [*(kv_pieces[k] for k in wave), weight, stats, wg, wg_from_before, wg_from_after, *dbars],
            [piece] * len(wave) + [struct((len(wave) * tokens_here, heads * rank), BF)],
            [pltpu.VMEM((heads, rank, pair), BF), pltpu.VMEM((heads, SEG, pair), FL)],
        )
        logit_grads.append(logit_grad)
        put(dkv_pieces, wave, exchange(dkv_send, devices, 1, wave))
    proj_send = call(
        bind(proj_kernel, waves),
        pos,
        [*kv_pieces, *logit_grads],
        [struct((heads * head_size // outer, rank), FL)] * outer,
        [pltpu.VMEM((heads * head_size, rank), FL)],
    )
    proj_parts = []
    for k in range(outer):
        place = [(o * inner + p, p * outer + (o ^ k)) for o in range(outer) for p in range(inner)]
        proj_parts.append(lax.ppermute(proj_send[k], "seq", place))
    whole = struct((tokens_here, row_width), BF)
    (grad_queries,) = call(
        bind(unpack_kernel), pos, dq_pieces, [whole], [pltpu.SemaphoreType.DMA((inner,))], far="outs"
    )
    sooner, later = waves[2] + waves[0], waves[1]
    grads = call(
        bind(unpack_pair_kernel, sooner, False),
        pos,
        [dkv_pieces[k] for k in sooner],
        [whole, whole],
        [pltpu.SemaphoreType.DMA((2 * len(sooner) * heads,))],
        far="outs",
    )
    count = len(later)
    grad_keys, grad_values, grad_proj = call(
        bind(unpack_pair_kernel, later, True),
        pos,
        [*(dkv_pieces[k] for k in later), *proj_parts, *grads],
        [whole, whole, struct(proj_parts[0].shape, FL)],
        [pltpu.SemaphoreType.DMA((2 * count * heads + 1,)), pltpu.VMEM(proj_parts[0].shape, FL)],
        far="outs",
        aliases=((count + outer, 0), (count + outer + 1, 1)),
    )
    return (grad_queries, grad_keys, grad_values, grad_proj)


def solution(mesh):
    in_specs = (P("seq", None), P("seq", None), P("seq", None), P("seq", None), P())
    out_specs = (P("seq", None), P("seq", None), P("seq", None), P("seq", None))
    return jax.shard_map(
        per_device, mesh=mesh, in_specs=in_specs, out_specs=out_specs, check_vma=False
    )
```
